32 devices in a mesh: rows: 8 (over z, y), sub: 4 (over x, core).
Axes of the slice: x: 2, y: 2, z: 4, core: 2. Of those that a mesh axis runs over, the one named last changes fastest.
Arguments:
- panel: float32 [12288, 256], P(('rows', 'sub'))
- trailing: float32 [12288, 1024], P(('rows', 'sub')), may hold values from -6 to 6
- live_rows: int32 [32], P(('rows', 'sub')), may hold values from 192 to 384, as said below
Outputs:
- basis: float32 [12288, 256], P(('rows', 'sub'))
- top_block: float32 [256, 1024], P(None, 'sub')
- remainder: float32 [12288, 1024], P(('rows', 'sub'))
The draws below stay inside these ranges and needn't reach their ends.
Inputs may be any that keep to these rules, and one draw needn't show every extreme that they name: `live_rows`: the live cells of a list are its first slots; the others are padding. Some list is full and some list holds exactly 192 cells.
All inputs are finite; a program needn't handle non-finite values.
Results may differ from the reference program's by a relative error of at most 0.00014.
Values sent between devices are 32-bit elements; how exact they have to be, the bound alone decides.
No kernel may reach another device: no remote copies, remote signals or barrier semaphores. Data moves between devices by JAX's collectives and lax.ppermute only.
A program may use at most 64 MiB of HBM per device.

```python
import math
import jax
import jax.numpy as jnp
from jax import lax

P_SIZE = 256
NEXT = 1024
ROWS_DEV = 384
LISTS = 32
CELLS = 12288


def draw_panel(key, part):
    keys = jax.random.split(jax.random.fold_in(key, 11), 3)
    values = jax.random.normal(keys[0], (CELLS, P_SIZE), jnp.float32)
    column_scale = jnp.exp(jax.random.uniform(keys[1], (1, P_SIZE), jnp.float32) * math.log(10.0))
    row_scale = jnp.exp(jax.random.uniform(keys[2], (CELLS, 1), jnp.float32) * math.log(4.0))
    return values * column_scale * row_scale


def draw_live_rows(key, part):
    keys = jax.random.split(jax.random.fold_in(key, 23), 2)
    lowest = ROWS_DEV // 2
    counts = jax.random.randint(keys[0], (LISTS,), lowest, ROWS_DEV + 1)
    order = jax.random.permutation(keys[1], LISTS)
    counts = counts.at[order[0]].set(ROWS_DEV)
    counts = counts.at[order[1]].set(lowest)
    return counts.astype(jnp.int32)


def level_of(key, dims, cuts, smallest, top_value):
    def one(dim, shards_of):
        steps = jax.random.uniform(jax.random.fold_in(jax.random.fold_in(key, 6), dim), (shards_of,), jnp.float32, smallest / len(cuts), top_value / len(cuts))
        return jnp.repeat(jnp.exp(steps), dims[dim] // shards_of).reshape((-1,) + (1,) * (len(dims) - dim - 1))

    loudness = one(*cuts[0])
    for cut in cuts[1:]:
        loudness = loudness * one(*cut)
    return loudness


def gaussian(key, dims, scale, bound, pieces=(), held_as=jnp.bfloat16):
    loudness = level_of(key, dims, pieces, -0.22, 0.18) if pieces else 1.0
    drawn = jax.random.normal(key, dims, jnp.float32) * scale * loudness
    return jnp.minimum(jnp.maximum(drawn, -bound), bound).astype(held_as)


def setup_inputs(seed: int = 0) -> dict:
    streams_of = jax.random.split(jax.random.key(seed), 4)
    return {
        "panel": draw_panel(jax.random.fold_in(streams_of[3], 71), 0),
        "trailing": gaussian(streams_of[1], (CELLS, NEXT), 1.0, 6.0, ((0, 32),), jnp.float32),
        "live_rows": draw_live_rows(jax.random.fold_in(streams_of[3], 71), 0),
    }


def reference(panel, trailing, live_rows):
    cells = panel.shape[0]
    row_index = jnp.arange(cells, dtype=jnp.int32)
    owner = row_index // ROWS_DEV
    live_mask = (row_index - owner * ROWS_DEV < live_rows[owner])[:, None]
    masked_panel = jnp.where(live_mask, panel, jnp.zeros_like(panel))
    masked_trail = jnp.where(live_mask, trailing, jnp.zeros_like(trailing))
    total = jnp.sum(live_rows).astype(jnp.float32)
    gram = jnp.dot(masked_panel.T.astype(jnp.float32), masked_panel.astype(jnp.float32), precision=lax.Precision.HIGHEST, preferred_element_type=jnp.float32)
    factor = jnp.linalg.cholesky(gram / total)
    basis = jax.scipy.linalg.solve_triangular(factor, masked_panel.T, lower=True).T
    root_total = jnp.sqrt(total)
    top_block = jnp.dot(basis.T.astype(jnp.float32), masked_trail.astype(jnp.float32), precision=lax.Precision.HIGHEST, preferred_element_type=jnp.float32) / root_total
    remainder = masked_trail - jnp.dot(basis.astype(jnp.float32), top_block.astype(jnp.float32), precision=lax.Precision.HIGHEST, preferred_element_type=jnp.float32) / root_total
    return (basis, top_block, remainder)
```

```python
import functools

import jax
import jax.numpy as jnp
from jax import lax
from jax.experimental import pallas as pl
from jax.experimental.pallas import tpu as pltpu
from jax.sharding import Mesh
from jax.sharding import PartitionSpec as P

CHIPS = ("z", "y", "x")
AXES = ("z", "y", "x", "core")
HIGHEST = lax.Precision.HIGHEST


def dot(left, right, contract, precision=HIGHEST):
    return lax.dot_general(
        left, right, (contract, ((), ())), precision=precision, preferred_element_type=jnp.float32
    )


def live_rows_mask(rows, live):
    return lax.broadcasted_iota(jnp.int32, (rows, 1), 0) < live


def products_kernel(core_ref, live_ref, panel_ref, trail_ref, keep_ref, send_ref):
    rows, width = panel_ref.shape
    half = width // 2
    live = live_ref[0]
    mine = live_rows_mask(rows, live)
    first = pl.multiple_of(core_ref[0] * half, half)
    second = pl.multiple_of((1 - core_ref[0]) * half, half)
    panel = jnp.where(mine, panel_ref[...], 0.0)
    trail = jnp.where(mine, trail_ref[...], 0.0)
    ordered = jnp.concatenate(
        [panel_ref[:, pl.ds(first, half)], panel_ref[:, pl.ds(second, half)]], axis=1
    )
    ordered = jnp.where(mine, ordered, 0.0)
    gram = dot(ordered, panel, ((0,), (0,)))
    cross = dot(ordered, trail, ((0,), (0,)))
    keep_ref[:, :width] = gram[:half]
    keep_ref[:, width:] = cross[:half]
    send_ref[:, :width] = gram[half:]
    send_ref[:, width:] = cross[half:]
    count = jnp.full((half, half), live, jnp.int32).astype(jnp.float32)

    @pl.when(core_ref[0] == 0)
    def _():
        keep_ref[:, half:width] = count

    @pl.when(core_ref[0] != 0)
    def _():
        send_ref[:, half:width] = count


def products(core, live, panel, trail):
    rows, width = panel.shape
    columns = width + trail.shape[1]
    out = jax.ShapeDtypeStruct((width // 2, columns), jnp.float32)
    return pl.pallas_call(
        products_kernel,
        out_shape=(out, out),
        in_specs=[
            pl.BlockSpec(memory_space=pltpu.SMEM),
            pl.BlockSpec(memory_space=pltpu.SMEM),
            pl.BlockSpec(memory_space=pltpu.VMEM),
            pl.BlockSpec(memory_space=pltpu.VMEM),
        ],
        out_specs=(pl.BlockSpec(memory_space=pltpu.VMEM),) * 2,
    )(core, live, panel, trail)


def final_kernel(
    core_ref, sub_ref, live_ref, total_ref, inverse_ref, own_ref, other_ref, panel_ref, trail_ref,
    basis_ref, top_ref, rest_ref, top_scr,
):
    rows, width = panel_ref.shape
    half = width // 2
    mine = live_rows_mask(rows, live_ref[0])
    panel = jnp.where(mine, panel_ref[...], 0.0)
    trail = jnp.where(mine, trail_ref[...], 0.0)
    first = pl.multiple_of(core_ref[0] * half, half)
    second = pl.multiple_of((1 - core_ref[0]) * half, half)
    unit = dot(panel, inverse_ref[...], ((1,), (1,)))
    basis_ref[...] = unit * jnp.sqrt(total_ref[0, 0])
    top = dot(inverse_ref[:, pl.ds(first, half)], own_ref[:, width:], ((1,), (0,))) + dot(
        inverse_ref[:, pl.ds(second, half)], other_ref[:, width:], ((1,), (0,))
    )
    top_scr[...] = top
    rest_ref[...] = trail - dot(unit, top, ((1,), (0,)))
    wide = top_ref.shape[1]
    top_ref[...] = top_scr[:, pl.ds(pl.multiple_of(sub_ref[0] * wide, wide), wide)]


def final(core, sub, live, total, inverse, own, other, panel, trail, wide):
    rows, width = panel.shape
    columns = trail.shape[1]
    f32 = jnp.float32
    return pl.pallas_call(
        final_kernel,
        out_shape=(
            jax.ShapeDtypeStruct((rows, width), f32),
            jax.ShapeDtypeStruct((width, wide), f32),
            jax.ShapeDtypeStruct((rows, columns), f32),
        ),
        in_specs=[pl.BlockSpec(memory_space=pltpu.SMEM)] * 3
        + [pl.BlockSpec(memory_space=pltpu.VMEM)] * 6,
        out_specs=(pl.BlockSpec(memory_space=pltpu.VMEM),) * 3,
        scratch_shapes=[pltpu.VMEM((width, columns), f32)],
    )(core, sub, live, total, inverse, own, other, panel, trail)


def swap(x):
    return lax.ppermute(x, "core", [(0, 1), (1, 0)])


def body(chips, panel, trailing, live_rows):
    width = panel.shape[1]
    half = width // 2
    core = lax.axis_index("core")
    sub = lax.axis_index("x") * 2 + core
    subs = lax.axis_size("x") * 2
    core_s, sub_s = core[None], sub[None]
    keep, send = products(core_s, live_rows, panel, trailing)
    mine = keep + swap(send)
    shape = mine.shape
    if half % chips == 0:
        chunks = mine.reshape(chips, half // chips, shape[1])
    else:
        chunks = mine.reshape(chips, -1)
    parts = lax.all_to_all(chunks, CHIPS, 0, 0, tiled=True)
    summed = jnp.broadcast_to(jnp.sum(parts, axis=0, keepdims=True), chunks.shape)
    own = lax.all_to_all(summed, CHIPS, 0, 0, tiled=True).reshape(shape)
    other = swap(own)
    low = jnp.where(core == 0, own[:, :width], other[:, :width])
    high = jnp.where(core == 0, other[:, :width], own[:, :width])
    total = low[0:1, half : half + 1]
    gram = jnp.concatenate(
        [jnp.concatenate([low[:, :half], high[:, :half].T], axis=1), high], axis=0
    )
    factor = jnp.linalg.cholesky(gram, symmetrize_input=False)
    inverse = jax.scipy.linalg.solve_triangular(factor, jnp.eye(width, dtype=jnp.float32), lower=True)
    return final(
        core_s, sub_s, live_rows, total, inverse, own, other, panel, trailing,
        trailing.shape[1] // subs,
    )


def solution(mesh):
    rows, subs = mesh.shape["rows"], mesh.shape["sub"]
    grid = Mesh(mesh.devices.reshape(rows // 2, 2, subs // 2, 2), AXES)
    chips = rows * subs // 2
    in_specs = (P(AXES, None), P(AXES, None), P(AXES))
    out_specs = (P(AXES, None), P(None, ("x", "core")), P(AXES, None))
    return jax.shard_map(
        functools.partial(body, chips),
        mesh=grid,
        in_specs=in_specs,
        out_specs=out_specs,
        check_vma=False,
    )
```

```python
import functools

import jax
import jax.numpy as jnp
from jax import lax
from jax.experimental import pallas as pl
from jax.experimental.pallas import tpu as pltpu
from jax.sharding import Mesh
from jax.sharding import PartitionSpec as P

AXES = ("far", "z", "y", "x", "core")
SLOTS = 4
PARTS = 4
HIGHEST = lax.Precision.HIGHEST
F32 = jnp.float32
BF16 = jnp.bfloat16
LANES = 128
BLOCK = 32
BATCH = 16
SMEM = pl.BlockSpec(memory_space=pltpu.SMEM)
VMEM = pl.BlockSpec(memory_space=pltpu.VMEM)
ANY = pl.BlockSpec(memory_space=pl.ANY)


def dot(left, right, contract):
    return lax.dot_general(
        left, right, (contract, ((), ())), precision=HIGHEST, preferred_element_type=F32
    )


def masked(ref, live_ref, columns=slice(None)):
    rows = ref.shape[0]
    live = lax.broadcasted_iota(jnp.int32, (rows, 1), 0) < live_ref[0]
    return jnp.where(live, ref[:, columns], 0.0)


def struct(*shape):
    return jax.ShapeDtypeStruct(shape, F32)


def cost(flops, transferred):
    return pl.CostEstimate(flops=flops, bytes_accessed=transferred, transcendentals=0)


def products_kernel(other, place_ref, live_ref, panel_ref, trail_ref, out_ref, cross_scr):
    rows, width = panel_ref.shape
    columns = trail_ref.shape[1]
    core, chip, depth = place_ref[0], place_ref[1], place_ref[2]
    side = 1 - core if other else core
    panel = masked(panel_ref, live_ref)
    tall = width // SLOTS
    part = width // PARTS
    half = masked(panel_ref, live_ref, pl.ds(pl.multiple_of(side * LANES, LANES), LANES))
    start = pl.multiple_of(side * (columns // 2), LANES)
    trail = masked(trail_ref, live_ref, pl.ds(start, columns // 2))
    product = dot(panel, jnp.concatenate([half, trail], axis=1), ((0,), (0,)))
    for tile in range(SLOTS + 1):
        cross_scr[tile] = product[:, tile * LANES : (tile + 1) * LANES]

    @pl.when(side == 0)
    def _():
        count = jnp.full((width - LANES, LANES), live_ref[0], jnp.int32)
        cross_scr[0, LANES:, :] = count.astype(F32)

    for slot in range(SLOTS):
        chunk = jnp.bitwise_xor(chip, slot)
        out_ref[slot, :tall, :] = cross_scr[0, pl.ds(pl.multiple_of(chunk * tall, 8), tall), :]
        for piece in range(PARTS):
            at = pl.multiple_of(jnp.bitwise_xor(depth, piece) * part, 8)
            to = tall + piece * part
            out_ref[slot, to : to + part, :] = cross_scr[chunk + 1, pl.ds(at, part), :]


def products_of(other, place, live, panel, trail):
    rows, width = panel.shape
    columns = trail.shape[1]
    return pl.pallas_call(
        functools.partial(products_kernel, other),
        out_shape=struct(SLOTS, width // SLOTS + width, LANES),
        in_specs=[SMEM, SMEM, VMEM, VMEM],
        out_specs=VMEM,
        scratch_shapes=[pltpu.VMEM((SLOTS + 1, width, LANES), F32)],
        cost_estimate=cost(12 * rows * width * (columns + width) // 2, 2 * rows * columns),
        name="products_other" if other else "products_own",
    )(place, live, panel, trail)


def parts_of(x):
    high = x.astype(BF16)
    rest = x - high.astype(F32)
    middle = rest.astype(BF16)
    return high, middle, (rest - middle.astype(F32)).astype(BF16)


def update_product(left, right):
    a, b, c = parts_of(left)
    d, e, f = parts_of(right)
    return lax.dot_general(
        jnp.concatenate([a, a, b, a, c, b], axis=0),
        jnp.concatenate([d, e, d, f, d, e], axis=0),
        (((0,), (0,)), ((), ())),
        preferred_element_type=F32,
    )


def across(x, lane):
    return jnp.broadcast_to(x[:, lane : lane + 1], (8, LANES))


def down(x, row):
    return jnp.broadcast_to(x[row : row + 1, :], (8, LANES))


def eliminate(rows, first):
    groups = len(rows)
    index = lax.broadcasted_iota(jnp.int32, (8, LANES), 0)
    pivots = [jnp.ones((8, LANES), F32) for _ in range(groups)]
    for start in range(0, BLOCK, BATCH):
        columns = {
            (group, j): across(rows[group][0], first + j)
            for j in range(start, start + BATCH)
            for group in range(j // 8, groups)
        }
        for j in range(start, start + BATCH):
            home, place = divmod(j, 8)
            pivot = down(columns[home, j], place)
            pivots[home] = jnp.where(index == place, pivot, pivots[home])
            inverse = 1.0 / pivot
            factors = {}
            for group in range(home, groups):
                column = columns[group, j]
                if group == home:
                    if place == 7:
                        continue
                    column = jnp.where(index > place, column, 0.0)
                factors[group] = column * inverse
            for m in range(j + 1, start + BATCH):
                value = down(columns[m // 8, j], m % 8)
                for group in range(m // 8, groups):
                    if group in factors:
                        columns[group, m] = columns[group, m] - factors[group] * value
            for tile in range(len(rows[0])):
                value = down(rows[home][tile], place)
                for group in factors:
                    rows[group][tile] = rows[group][tile] - factors[group] * value
    return pivots


def factor_inverse(gram_ref, inverse_ref):
    size = gram_ref.shape[0]
    row = lax.broadcasted_iota(jnp.int32, (size, size), 0)
    column = lax.broadcasted_iota(jnp.int32, (size, size), 1)
    inverse_ref[...] = jnp.where(row == column, 1.0, 0.0)
    tiles = size // LANES
    groups = BLOCK // 8

    def tile_of(index):
        return slice(index * LANES, (index + 1) * LANES)

    for start in range(0, size, BLOCK):
        stop = start + BLOCK
        here = start // LANES
        rows = []
        for group in range(groups):
            at = slice(start + 8 * group, start + 8 * group + 8)
            rows.append(
                [gram_ref[at, tile_of(t)] for t in range(here, tiles)]
                + [inverse_ref[at, tile_of(t)] for t in range(here + 1)]
            )
        pivots = eliminate(rows, start % LANES)
        for group in range(groups):
            scale = lax.rsqrt(pivots[group])
            rows[group] = [value * scale for value in rows[group]]
            at = slice(start + 8 * group, start + 8 * group + 8)
            for t in range(here + 1):
                inverse_ref[at, tile_of(t)] = rows[group][tiles - here + t]
        if stop == size:
            break
        base = stop // LANES
        stacked = [
            jnp.concatenate([rows[group][i] for group in range(groups)], axis=0)
            for i in range(base - here, len(rows[0]))
        ]
        left = jnp.concatenate(stacked[: tiles - base], axis=1)
        product = update_product(left, jnp.concatenate(stacked, axis=1))[stop - base * LANES :]
        for i, t in enumerate(range(base, tiles)):
            gram_ref[stop:, tile_of(t)] -= product[:, tile_of(i)]
        for t in range(here + 1):
            inverse_ref[stop:, tile_of(t)] -= product[:, tile_of(tiles - base + t)]


def factor_kernel(
    place_ref, live_ref, own_ref, other_ref, panel_ref, inverse_ref, unit_ref, basis_ref, gram_ref
):
    core, chip = place_ref[0], place_ref[1]
    tall = own_ref.shape[1]
    for side, ref in ((core, own_ref), (1 - core, other_ref)):
        at = pl.ds(pl.multiple_of(side * LANES, LANES), LANES)
        for slot in range(SLOTS):
            row = pl.multiple_of(jnp.bitwise_xor(chip, slot) * tall, 8)
            gram_ref[pl.ds(row, tall), at] = ref[slot]
    root = jnp.sqrt(gram_ref[LANES : LANES + 8, 0:LANES])[0:1, 0:1]
    factor_inverse(gram_ref, inverse_ref)
    unit = dot(masked(panel_ref, live_ref), inverse_ref[...], ((1,), (1,)))
    unit_ref[...] = unit
    basis_ref[...] = unit * root


def factor_of(place, live, own, other, panel):
    rows, width = panel.shape
    return pl.pallas_call(
        factor_kernel,
        out_shape=(struct(width, width), struct(rows, width), struct(rows, width)),
        in_specs=[SMEM, SMEM, VMEM, VMEM, VMEM],
        out_specs=(VMEM,) * 3,
        scratch_shapes=[pltpu.VMEM((width, width), F32)],
        cost_estimate=cost(6 * 10**9, 4 * rows * width),
        name="factor",
    )(place, live, own, other, panel)


def rest_kernel(other, place_ref, live_ref, inverse_ref, unit_ref, cross_ref, trail_ref, *refs):
    width = inverse_ref.shape[0]
    half = trail_ref.shape[1] // 2
    core, chip, depth = place_ref[0], place_ref[1], place_ref[2]
    if other:
        top_before_ref, _, top_ref, rest_ref, top_scr, cross_scr, rest_scr, sem = refs
        side = 1 - core
    else:
        top_ref, rest_ref, top_scr, cross_scr, rest_scr, sem = refs
        side = core
    start = pl.multiple_of(side * half, half)
    part = width // PARTS
    for slot in range(SLOTS):
        lane = pl.multiple_of(jnp.bitwise_xor(chip, slot) * LANES, LANES)
        for piece in range(PARTS):
            row = pl.multiple_of(jnp.bitwise_xor(depth, piece) * part, 8)
            cross_scr[pl.ds(row, part), pl.ds(lane, LANES)] = cross_ref[
                slot, piece * part : (piece + 1) * part, :
            ]
    top = dot(inverse_ref[...], cross_scr[...], ((1,), (0,)))
    rest_scr[...] = masked(trail_ref, live_ref, pl.ds(start, half)) - dot(
        unit_ref[...], top, ((1,), (0,))
    )
    copy = pltpu.make_async_copy(rest_scr, rest_ref.at[:, pl.ds(start, half)], sem)
    copy.start()
    top_scr[...] = top
    wide = top_ref.shape[1]
    mine = top_scr[:, pl.ds(pl.multiple_of(place_ref[4], LANES), wide)]
    if other:
        top_ref[...] = jnp.where(place_ref[3] == side, mine, top_before_ref[...])
    else:
        top_ref[...] = mine
    copy.wait()


def rest_of(other, place, live, inverse, unit, cross, trail, wide, before):
    rows, width = unit.shape
    columns = trail.shape[1]
    half = columns // 2
    return pl.pallas_call(
        functools.partial(rest_kernel, other),
        out_shape=(struct(width, wide), struct(rows, columns)),
        in_specs=[SMEM] * 2 + [VMEM] * 4 + ([VMEM, ANY] if other else []),
        out_specs=(VMEM, ANY),
        scratch_shapes=[
            pltpu.VMEM((width, half), F32),
            pltpu.VMEM((width, half), F32),
            pltpu.VMEM((rows, half), F32),
            pltpu.SemaphoreType.DMA,
        ],
        input_output_aliases={7: 1} if other else {},
        cost_estimate=cost(12 * (rows + width) * width * half, 8 * rows * half),
        name="rest_other" if other else "rest_own",
    )(place, live, inverse, unit, cross, trail, *before)


def swap(x):
    return lax.ppermute(x, "core", [(0, 1), (1, 0)])


def send(x, axes, size, shift):
    return lax.ppermute(x, axes, [(i, i ^ shift) for i in range(size)])


def tree(parts):
    return (parts[0] + parts[1]) + (parts[2] + parts[3])


def body(panel, trailing, live_rows):
    width, columns = panel.shape[1], trailing.shape[1]
    flat, deep = ("y", "x"), "z"
    core = lax.axis_index("core")
    wide = columns // (lax.axis_size("x") * 2)
    begin = (lax.axis_index("x") * 2 + core) * wide
    side = begin // (columns // 2)
    place = jnp.stack(
        [
            core,
            lax.axis_index(flat),
            lax.axis_index(deep),
            side,
            begin - side * (columns // 2),
        ]
    )
    tall, part = width // SLOTS, width // PARTS

    theirs = products_of(True, place, live_rows, panel, trailing)
    ours = products_of(False, place, live_rows, panel, trailing)
    pair = ours + swap(theirs)
    slots = [pair[0]] + [send(pair[k], flat, SLOTS, k) for k in range(1, SLOTS)]
    summed = tree(slots)
    gram = summed[:tall]
    pieces = [
        jnp.concatenate([gram, summed[tall + j * part : tall + (j + 1) * part]])
        for j in range(PARTS)
    ]
    pieces = [pieces[0]] + [send(pieces[j], deep, PARTS, j) for j in range(1, PARTS)]
    summed = tree(pieces)
    if lax.axis_size("far") > 1:
        summed = lax.psum(summed, "far")
    gram, cross = summed[:tall], summed[tall:]
    gram_own = jnp.stack([gram] + [send(gram, flat, SLOTS, k) for k in range(1, SLOTS)])
    cross = jnp.concatenate([cross] + [send(cross, deep, PARTS, j) for j in range(1, PARTS)])
    cross_own = [cross] + [send(cross, flat, SLOTS, k) for k in range(1, SLOTS)]
    inverse, unit, basis = factor_of(place, live_rows, gram_own, swap(gram_own), panel)
    *cross_own, inverse = lax.optimization_barrier((*cross_own, inverse))
    cross_own = jnp.stack(cross_own)
    cross_other = swap(cross_own)
    args = (place, live_rows, inverse, unit)
    before = rest_of(False, *args, cross_own, trailing, wide, ())
    top, rest = rest_of(True, *args, cross_other, trailing, wide, before)
    return basis, top, rest


def solution(mesh):
    rows, subs = mesh.shape["rows"], mesh.shape["sub"]
    grid = Mesh(mesh.devices.reshape(rows // (2 * PARTS), PARTS, 2, subs // 2, 2), AXES)
    in_specs = (P(AXES, None), P(AXES, None), P(AXES))
    out_specs = (P(AXES, None), P(None, ("x", "core")), P(AXES, None))
    return jax.shard_map(
        body, mesh=grid, in_specs=in_specs, out_specs=out_specs, check_vma=False
    )
```

```python
import functools

import jax
import jax.numpy as jnp
from jax import lax
from jax.experimental import pallas as pl
from jax.experimental.pallas import tpu as pltpu
from jax.sharding import Mesh
from jax.sharding import PartitionSpec as P

AXES = ("far", "z", "y", "x", "core")
SLOTS = 4
PARTS = 4
F32 = jnp.float32
BF16 = jnp.bfloat16
LANES = 128
BLOCK = 32
BATCH = 16
SMEM = pl.BlockSpec(memory_space=pltpu.SMEM)
VMEM = pl.BlockSpec(memory_space=pltpu.VMEM)
ANY = pl.BlockSpec(memory_space=pl.ANY)
PARAMS = pltpu.CompilerParams(vmem_limit_bytes=16 << 20)


def place_of(ref):
    number = ref[0]
    return number % 2, number // 2 % SLOTS, number // (2 * SLOTS) % PARTS


def parts_of(x):
    high = x.astype(BF16)
    rest = x - high.astype(F32)
    middle = rest.astype(BF16)
    return high, middle, (rest - middle.astype(F32)).astype(BF16)


def left_of(x, axis, count=3):
    a, b, c = parts_of(x)
    return jnp.concatenate([a, a, b, a, c, b][:count], axis=axis)


def right_of(x, count=3):
    a, b, c = parts_of(x)
    return jnp.concatenate([a, b, a, c, a, b][:count], axis=0)


def dot(left, right, contract=((1,), (0,))):
    return lax.dot_general(left, right, (contract, ((), ())), preferred_element_type=F32)


def masked(ref, live_ref, columns=slice(None)):
    rows = ref.shape[0]
    live = lax.broadcasted_iota(jnp.int32, (rows, 1), 0) < live_ref[0]
    return jnp.where(live, ref[:, columns], 0.0)


def struct(*shape):
    return jax.ShapeDtypeStruct(shape, F32)


def cost(flops, transferred):
    return pl.CostEstimate(flops=flops, bytes_accessed=transferred, transcendentals=0)


def products_kernel(other, place_ref, live_ref, panel_ref, trail_ref, out_ref, cross_scr):
    rows, width = panel_ref.shape
    columns = trail_ref.shape[1]
    core, chip, depth = place_of(place_ref)
    side = 1 - core if other else core
    tall = width // SLOTS
    part = width // PARTS
    half = masked(panel_ref, live_ref, pl.ds(pl.multiple_of(side * LANES, LANES), LANES))
    start = pl.multiple_of(side * (columns // 2), LANES)
    trail = masked(trail_ref, live_ref, pl.ds(start, columns // 2))
    panel = left_of(masked(panel_ref, live_ref).T, 1, 6)
    cross_scr[0] = dot(panel, right_of(half, 6))
    product = dot(panel[:, : 3 * rows], right_of(trail))
    for tile in range(SLOTS):
        cross_scr[tile + 1] = product[:, tile * LANES : (tile + 1) * LANES]

    @pl.when(side == 0)
    def _():
        count = jnp.full((width - LANES, LANES), live_ref[0], jnp.int32)
        cross_scr[0, LANES:, :] = count.astype(F32)

    for slot in range(SLOTS):
        chunk = jnp.bitwise_xor(chip, slot)
        out_ref[slot, :tall, :] = cross_scr[0, pl.ds(pl.multiple_of(chunk * tall, 8), tall), :]
        for piece in range(PARTS):
            at = pl.multiple_of(jnp.bitwise_xor(depth, piece) * part, 8)
            to = tall + piece * part
            out_ref[slot, to : to + part, :] = cross_scr[chunk + 1, pl.ds(at, part), :]


def products_of(other, place, live, panel, trail):
    rows, width = panel.shape
    columns = trail.shape[1]
    return pl.pallas_call(
        functools.partial(products_kernel, other),
        out_shape=struct(SLOTS, width // SLOTS + width, LANES),
        in_specs=[SMEM, SMEM, VMEM, VMEM],
        out_specs=VMEM,
        scratch_shapes=[pltpu.VMEM((SLOTS + 1, width, LANES), F32)],
        cost_estimate=cost(12 * rows * width * (columns + width) // 2, 2 * rows * columns),
        compiler_params=PARAMS,
        name="products_other" if other else "products_own",
    )(place, live, panel, trail)


def across(x, lane):
    return jnp.broadcast_to(x[:, lane : lane + 1], (8, LANES))


def down(x, row):
    return jnp.broadcast_to(x[row : row + 1, :], (8, LANES))


def eliminate(rows, first):
    groups = len(rows)
    index = lax.broadcasted_iota(jnp.int32, (8, LANES), 0)
    pivots = [jnp.ones((8, LANES), F32) for _ in range(groups)]
    for start in range(0, BLOCK, BATCH):
        columns = {
            (group, j): across(rows[group][0], first + j)
            for j in range(start, start + BATCH)
            for group in range(j // 8, groups)
        }
        for j in range(start, start + BATCH):
            home, place = divmod(j, 8)
            pivot = down(columns[home, j], place)
            pivots[home] = jnp.where(index == place, pivot, pivots[home])
            inverse = 1.0 / pivot
            factors = {}
            for group in range(home, groups):
                column = columns[group, j]
                if group == home:
                    if place == 7:
                        continue
                    column = jnp.where(index > place, column, 0.0)
                factors[group] = column * inverse
            for m in range(j + 1, start + BATCH):
                value = down(columns[m // 8, j], m % 8)
                for group in range(m // 8, groups):
                    if group in factors:
                        columns[group, m] = columns[group, m] - factors[group] * value
            for tile in range(len(rows[0])):
                value = down(rows[home][tile], place)
                for group in factors:
                    rows[group][tile] = rows[group][tile] - factors[group] * value
    return pivots


def factor_inverse(gram_ref, inverse_ref):
    size = gram_ref.shape[0]
    row = lax.broadcasted_iota(jnp.int32, (size, size), 0)
    column = lax.broadcasted_iota(jnp.int32, (size, size), 1)
    inverse_ref[...] = jnp.where(row == column, 1.0, 0.0)
    tiles = size // LANES
    groups = BLOCK // 8

    def tile_of(index):
        return slice(index * LANES, (index + 1) * LANES)

    for start in range(0, size, BLOCK):
        stop = start + BLOCK
        here = start // LANES
        rows = []
        for group in range(groups):
            at = slice(start + 8 * group, start + 8 * group + 8)
            rows.append(
                [gram_ref[at, tile_of(t)] for t in range(here, tiles)]
                + [inverse_ref[at, tile_of(t)] for t in range(here + 1)]
            )
        pivots = eliminate(rows, start % LANES)
        for group in range(groups):
            scale = lax.rsqrt(pivots[group])
            rows[group] = [value * scale for value in rows[group]]
            at = slice(start + 8 * group, start + 8 * group + 8)
            for t in range(here + 1):
                inverse_ref[at, tile_of(t)] = rows[group][tiles - here + t]
        if stop == size:
            break
        base = stop // LANES
        stacked = [
            jnp.concatenate([rows[group][i] for group in range(groups)], axis=0)
            for i in range(base - here, len(rows[0]))
        ]
        left = jnp.concatenate(stacked[: tiles - base], axis=1)
        product = dot(
            left_of(left, 0, 6), right_of(jnp.concatenate(stacked, axis=1), 6), ((0,), (0,))
        )[stop - base * LANES :]
        for i, t in enumerate(range(base, tiles)):
            gram_ref[stop:, tile_of(t)] -= product[:, tile_of(i)]
        for t in range(here + 1):
            inverse_ref[stop:, tile_of(t)] -= product[:, tile_of(tiles - base + t)]


def factor_kernel(
    place_ref, live_ref, own_ref, other_ref, panel_ref, left_ref, unit_ref, basis_ref,
    gram_ref, inverse_ref,
):
    core, chip, _ = place_of(place_ref)
    tall = own_ref.shape[1]
    for side, ref in ((core, own_ref), (1 - core, other_ref)):
        at = pl.ds(pl.multiple_of(side * LANES, LANES), LANES)
        for slot in range(SLOTS):
            row = pl.multiple_of(jnp.bitwise_xor(chip, slot) * tall, 8)
            gram_ref[pl.ds(row, tall), at] = ref[slot]
    root = jnp.sqrt(gram_ref[LANES : LANES + 8, 0:LANES])[0:1, 0:1]
    factor_inverse(gram_ref, inverse_ref)
    inverse = inverse_ref[...]
    left_ref[...] = left_of(inverse, 1)
    unit = dot(left_of(masked(panel_ref, live_ref), 1), right_of(inverse.T))
    unit_ref[...] = left_of(unit, 1)
    basis_ref[...] = unit * root


def factor_of(place, live, own, other, panel):
    rows, width = panel.shape
    return pl.pallas_call(
        factor_kernel,
        out_shape=(
            jax.ShapeDtypeStruct((width, 3 * width), BF16),
            jax.ShapeDtypeStruct((rows, 3 * width), BF16),
            struct(rows, width),
        ),
        in_specs=[SMEM, SMEM, VMEM, VMEM, VMEM],
        out_specs=(VMEM,) * 3,
        scratch_shapes=[pltpu.VMEM((width, width), F32)] * 2,
        cost_estimate=cost(6 * 10**9, 4 * rows * width),
        compiler_params=PARAMS,
        name="factor",
    )(place, live, own, other, panel)


def rest_kernel(other, place_ref, live_ref, inverse_ref, unit_ref, cross_ref, trail_ref, *refs):
    width = inverse_ref.shape[0]
    columns = trail_ref.shape[1]
    half = columns // 2
    core, chip, depth = place_of(place_ref)
    if other:
        top_before_ref, _, top_ref, rest_ref, top_scr, cross_scr, rest_scr, sem = refs
        side = 1 - core
    else:
        top_ref, rest_ref, top_scr, cross_scr, rest_scr, sem = refs
        side = core
    start = pl.multiple_of(side * half, half)
    part = width // PARTS
    for slot in range(SLOTS):
        lane = pl.multiple_of(jnp.bitwise_xor(chip, slot) * LANES, LANES)
        for piece in range(PARTS):
            row = pl.multiple_of(jnp.bitwise_xor(depth, piece) * part, 8)
            cross_scr[pl.ds(row, part), pl.ds(lane, LANES)] = cross_ref[
                slot, piece * part : (piece + 1) * part, :
            ]
    top = dot(inverse_ref[...], right_of(cross_scr[...]))
    rest_scr[...] = masked(trail_ref, live_ref, pl.ds(start, half)) - dot(
        unit_ref[...], right_of(top)
    )
    copy = pltpu.make_async_copy(rest_scr, rest_ref.at[:, pl.ds(start, half)], sem)
    copy.start()
    top_scr[...] = top
    wide = top_ref.shape[1]
    begin = place_ref[0] % (columns // wide) * wide
    mine = top_scr[:, pl.ds(pl.multiple_of(begin % half, LANES), wide)]
    if other:
        top_ref[...] = jnp.where(begin // half == side, mine, top_before_ref[...])
    else:
        top_ref[...] = mine
    copy.wait()


def rest_of(other, place, live, inverse, unit, cross, trail, wide, before):
    rows, columns = trail.shape
    width = inverse.shape[0]
    half = columns // 2
    return pl.pallas_call(
        functools.partial(rest_kernel, other),
        out_shape=(struct(width, wide), struct(rows, columns)),
        in_specs=[SMEM] * 2 + [VMEM] * 4 + ([VMEM, ANY] if other else []),
        out_specs=(VMEM, ANY),
        scratch_shapes=[
            pltpu.VMEM((width, half), F32),
            pltpu.VMEM((width, half), F32),
            pltpu.VMEM((rows, half), F32),
            pltpu.SemaphoreType.DMA,
        ],
        input_output_aliases={7: 1} if other else {},
        cost_estimate=cost(12 * (rows + width) * width * half, 8 * rows * half),
        compiler_params=PARAMS,
        name="rest_other" if other else "rest_own",
    )(place, live, inverse, unit, cross, trail, *before)


def swap(x):
    return lax.ppermute(x, "core", [(0, 1), (1, 0)])


def send(x, axes, size, shift):
    return lax.ppermute(x, axes, [(i, i ^ shift) for i in range(size)])


def tree(parts):
    return (parts[0] + parts[1]) + (parts[2] + parts[3])


def body(panel, trailing, live_rows):
    width, columns = panel.shape[1], trailing.shape[1]
    flat, deep = ("y", "x"), "z"
    wide = columns // (lax.axis_size("x") * 2)
    place = lax.axis_index(AXES)[None]
    tall, part = width // SLOTS, width // PARTS

    theirs = products_of(True, place, live_rows, panel, trailing)
    ours = products_of(False, place, live_rows, panel, trailing)
    pair = ours + swap(theirs)
    slots = [pair[0]] + [send(pair[k], flat, SLOTS, k) for k in range(1, SLOTS)]
    summed = tree(slots)
    gram = summed[:tall]
    pieces = [
        jnp.concatenate([gram, summed[tall + j * part : tall + (j + 1) * part]])
        for j in range(PARTS)
    ]
    pieces = [pieces[0]] + [send(pieces[j], deep, PARTS, j) for j in range(1, PARTS)]
    summed = tree(pieces)
    if lax.axis_size("far") > 1:
        summed = lax.psum(summed, "far")
    gram, cross = summed[:tall], summed[tall:]
    gram_own = jnp.stack([gram] + [send(gram, flat, SLOTS, k) for k in range(1, SLOTS)])
    cross = jnp.concatenate([cross] + [send(cross, deep, PARTS, j) for j in range(1, PARTS)])
    cross_own = [cross] + [send(cross, flat, SLOTS, k) for k in range(1, SLOTS)]
    inverse, unit, basis = factor_of(place, live_rows, gram_own, swap(gram_own), panel)
    *cross_own, inverse = lax.optimization_barrier((*cross_own, inverse))
    cross_own = jnp.stack(cross_own)
    cross_other = swap(cross_own)
    args = (place, live_rows, inverse, unit)
    before = rest_of(False, *args, cross_own, trailing, wide, ())
    top, rest = rest_of(True, *args, cross_other, trailing, wide, before)
    return basis, top, rest


def solution(mesh):
    rows, subs = mesh.shape["rows"], mesh.shape["sub"]
    grid = Mesh(mesh.devices.reshape(rows // (2 * PARTS), PARTS, 2, subs // 2, 2), AXES)
    in_specs = (P(AXES, None), P(AXES, None), P(AXES))
    out_specs = (P(AXES, None), P(None, ("x", "core")), P(AXES, None))
    return jax.shard_map(
        body, mesh=grid, in_specs=in_specs, out_specs=out_specs, check_vma=False
    )
```

```python
import functools

import jax
import jax.numpy as jnp
from jax import lax
from jax.experimental import pallas as pl
from jax.experimental.pallas import tpu as pltpu
from jax.sharding import Mesh
from jax.sharding import PartitionSpec as P

AXES = ("far", "z", "y", "x", "core")
SLOTS = 4
PARTS = 4
F32 = jnp.float32
BF16 = jnp.bfloat16
LANES = 128
BLOCK = 32
BATCH = 16
STRIP = 256
SMEM = pl.BlockSpec(memory_space=pltpu.SMEM)
VMEM = pl.BlockSpec(memory_space=pltpu.VMEM)
ANY = pl.BlockSpec(memory_space=pl.ANY)
HBM = pl.BlockSpec(memory_space=pltpu.HBM)
PARAMS = pltpu.CompilerParams(vmem_limit_bytes=16 << 20)


def in_hbm(x):
    return pltpu.with_memory_space_constraint(x, pltpu.HBM)


def place_of(ref):
    number = ref[0]
    return number % 2, number // 2 % SLOTS, number // (2 * SLOTS) % PARTS


def parts_of(x):
    high = x.astype(BF16)
    rest = x - high.astype(F32)
    middle = rest.astype(BF16)
    return high, middle, (rest - middle.astype(F32)).astype(BF16)


def left_of(x, axis, count=3):
    a, b, c = parts_of(x)
    return jnp.concatenate([a, a, b, a, c, b][:count], axis=axis)


def right_of(x, count=3, axis=0):
    a, b, c = parts_of(x)
    return jnp.concatenate([a, b, a, c, a, b][:count], axis=axis)


def dot(left, right, contract=((1,), (0,))):
    return lax.dot_general(left, right, (contract, ((), ())), preferred_element_type=F32)


def masked(ref, live_ref, columns=slice(None)):
    rows = ref.shape[0]
    live = lax.broadcasted_iota(jnp.int32, (rows, 1), 0) < live_ref[0]
    return jnp.where(live, ref[:, columns], 0.0)


def struct(*shape):
    return jax.ShapeDtypeStruct(shape, F32)


def cost(flops, transferred):
    return pl.CostEstimate(flops=flops, bytes_accessed=transferred, transcendentals=0)


def place_products(side, place_ref, live_ref, gram, cross, out_ref, cross_scr):
    width = gram.shape[0]
    _, chip, depth = place_of(place_ref)
    tall = width // SLOTS
    part = width // PARTS
    cross_scr[0] = gram
    for tile in range(SLOTS):
        cross_scr[tile + 1] = cross[:, tile * LANES : (tile + 1) * LANES]

    @pl.when(side == 0)
    def _():
        count = jnp.full((width - LANES, LANES), live_ref[0], jnp.int32)
        cross_scr[0, LANES:, :] = count.astype(F32)

    for slot in range(SLOTS):
        chunk = jnp.bitwise_xor(chip, slot)
        out_ref[slot, :tall, :] = cross_scr[0, pl.ds(pl.multiple_of(chunk * tall, 8), tall), :]
        for piece in range(PARTS):
            at = pl.multiple_of(jnp.bitwise_xor(depth, piece) * part, 8)
            to = tall + piece * part
            out_ref[slot, to : to + part, :] = cross_scr[chunk + 1, pl.ds(at, part), :]


def other_kernel(
    place_ref, live_ref, panel_ref, trail_ref, out_ref, left_ref, gram_ref, half_ref,
    cross_scr, panel_scr, trail_scr, panel_sem, trail_sem, half_sem,
):
    columns = trail_ref.shape[1]
    core = place_of(place_ref)[0]
    wide = columns // 2

    def columns_of(side):
        return trail_ref.at[:, pl.ds(pl.multiple_of(side * wide, LANES), wide)]

    copy_panel = pltpu.make_async_copy(panel_ref, panel_scr, panel_sem)
    copy_trail = pltpu.make_async_copy(columns_of(1 - core), trail_scr, trail_sem)
    copy_half = pltpu.make_async_copy(columns_of(core), half_ref, half_sem)
    copy_panel.start()
    copy_trail.start()
    copy_half.start()
    copy_panel.wait()
    rows = panel_scr.shape[0]
    panel = masked(panel_scr, live_ref)
    left = left_of(panel.T, 1, 6)
    left_ref[...] = left[:, : 3 * rows]
    gram = dot(left, right_of(panel, 6))
    panel_scr[: gram.shape[0], :] = gram
    own = pl.ds(pl.multiple_of(core * LANES, LANES), LANES)
    rest = pl.ds(pl.multiple_of((1 - core) * LANES, LANES), LANES)
    gram_ref[...] = panel_scr[: gram.shape[0], own]
    copy_trail.wait()
    cross = dot(left[:, : 3 * rows], right_of(masked(trail_scr, live_ref)))
    gram = panel_scr[: gram.shape[0], rest]
    place_products(1 - core, place_ref, live_ref, gram, cross, out_ref, cross_scr)
    copy_half.wait()


def own_kernel(place_ref, live_ref, left_ref, gram_ref, half_ref, out_ref, cross_scr):
    cross = dot(left_ref[...], right_of(masked(half_ref, live_ref)))
    side = place_of(place_ref)[0]
    place_products(side, place_ref, live_ref, gram_ref[...], cross, out_ref, cross_scr)


def products_of(place, live, panel, trail):
    rows, width = panel.shape
    columns = trail.shape[1]
    out = struct(SLOTS, width // SLOTS + width, LANES)
    work = cost(6 * rows * width * columns // 2, 2 * rows * columns)
    cross_scr = pltpu.VMEM((SLOTS + 1, width, LANES), F32)
    theirs, *handed = pl.pallas_call(
        other_kernel,
        out_shape=(
            out,
            jax.ShapeDtypeStruct((width, 3 * rows), BF16),
            struct(width, LANES),
            struct(rows, columns // 2),
        ),
        in_specs=[SMEM, SMEM, HBM, HBM],
        out_specs=(VMEM,) * 4,
        scratch_shapes=[
            cross_scr,
            pltpu.VMEM((rows, width), F32),
            pltpu.VMEM((rows, columns // 2), F32),
        ]
        + [pltpu.SemaphoreType.DMA] * 3,
        cost_estimate=work,
        compiler_params=PARAMS,
        name="products_other",
    )(place, live, in_hbm(panel), in_hbm(trail))
    ours = pl.pallas_call(
        own_kernel,
        out_shape=out,
        in_specs=[SMEM, SMEM] + [VMEM] * 3,
        out_specs=VMEM,
        scratch_shapes=[cross_scr],
        cost_estimate=work,
        compiler_params=PARAMS,
        name="products_own",
    )(place, live, *handed)
    return theirs, ours


def across(x, lane):
    return jnp.broadcast_to(x[:, lane : lane + 1], (8, LANES))


def down(x, row):
    return jnp.broadcast_to(x[row : row + 1, :], (8, LANES))


def eliminate(rows, first):
    groups = len(rows)
    index = lax.broadcasted_iota(jnp.int32, (8, LANES), 0)
    pivots = [jnp.ones((8, LANES), F32) for _ in range(groups)]
    for start in range(0, BLOCK, BATCH):
        columns = {
            (group, j): across(rows[group][0], first + j)
            for j in range(start, start + BATCH)
            for group in range(j // 8, groups)
        }
        for j in range(start, start + BATCH, 2):
            home, place = divmod(j, 8)
            a = down(columns[home, j], place)
            b = down(columns[home, j], place + 1)
            c = down(columns[home, j + 1], place + 1)
            minor = a * c - b * b
            over_a, over_minor = 1.0 / a, 1.0 / minor
            ratio = b * over_a
            pivots[home] = jnp.where(index == place, a, pivots[home])
            pivots[home] = jnp.where(index == place + 1, minor * over_a, pivots[home])
            first_factor, second_factor = {}, {}
            for group in range(home, groups):
                one = columns[group, j]
                two = columns[group, j + 1] * a - one * b
                if group == home:
                    one = jnp.where(index > place, one, 0.0)
                    two = jnp.where(index > place + 1, two, 0.0)
                first_factor[group] = one * over_a
                second_factor[group] = two * over_minor
            for m in range(j + 2, start + BATCH):
                value = down(columns[m // 8, j], m % 8)
                other = down(columns[m // 8, j + 1], m % 8) - ratio * value
                for group in range(m // 8, groups):
                    columns[group, m] = (
                        columns[group, m]
                        - first_factor[group] * value
                        - second_factor[group] * other
                    )
            for tile in range(len(rows[0])):
                value = down(rows[home][tile], place)
                other = down(rows[home][tile], place + 1) - ratio * value
                for group in first_factor:
                    rows[group][tile] = (
                        rows[group][tile]
                        - first_factor[group] * value
                        - second_factor[group] * other
                    )
    return pivots


def factor_inverse(gram_ref, inverse_ref):
    size = gram_ref.shape[0]
    row = lax.broadcasted_iota(jnp.int32, (size, size), 0)
    column = lax.broadcasted_iota(jnp.int32, (size, size), 1)
    inverse_ref[...] = jnp.where(row == column, 1.0, 0.0)
    tiles = size // LANES
    groups = BLOCK // 8

    def tile_of(index):
        return slice(index * LANES, (index + 1) * LANES)

    for start in range(0, size, BLOCK):
        stop = start + BLOCK
        here = start // LANES
        rows = []
        for group in range(groups):
            at = slice(start + 8 * group, start + 8 * group + 8)
            rows.append(
                [gram_ref[at, tile_of(t)] for t in range(here, tiles)]
                + [inverse_ref[at, tile_of(t)] for t in range(here + 1)]
            )
        pivots = eliminate(rows, start % LANES)
        for group in range(groups):
            scale = lax.rsqrt(pivots[group])
            rows[group] = [value * scale for value in rows[group]]
            at = slice(start + 8 * group, start + 8 * group + 8)
            for t in range(here + 1):
                inverse_ref[at, tile_of(t)] = rows[group][tiles - here + t]
        if stop == size:
            break
        base = stop // LANES
        stacked = [
            jnp.concatenate([rows[group][i] for group in range(groups)], axis=0)
            for i in range(base - here, len(rows[0]))
        ]
        left = jnp.concatenate(stacked[: tiles - base], axis=1)
        product = dot(
            left_of(left, 0, 6), right_of(jnp.concatenate(stacked, axis=1), 6), ((0,), (0,))
        )[stop - base * LANES :]
        for i, t in enumerate(range(base, tiles)):
            gram_ref[stop:, tile_of(t)] -= product[:, tile_of(i)]
        for t in range(here + 1):
            inverse_ref[stop:, tile_of(t)] -= product[:, tile_of(tiles - base + t)]


def factor_kernel(
    place_ref, live_ref, own_ref, other_ref, panel_ref, left_ref, unit_ref, basis_ref,
    gram_ref, inverse_ref,
):
    core, chip, _ = place_of(place_ref)
    tall = own_ref.shape[1]
    for side, ref in ((core, own_ref), (1 - core, other_ref)):
        at = pl.ds(pl.multiple_of(side * LANES, LANES), LANES)
        for slot in range(SLOTS):
            row = pl.multiple_of(jnp.bitwise_xor(chip, slot) * tall, 8)
            gram_ref[pl.ds(row, tall), at] = ref[slot]
    root = jnp.sqrt(gram_ref[LANES : LANES + 8, 0:LANES])[0:1, 0:1]
    factor_inverse(gram_ref, inverse_ref)
    inverse = inverse_ref[...]
    left_ref[...] = left_of(inverse, 1)
    unit = dot(left_of(masked(panel_ref, live_ref), 1), right_of(inverse, axis=1), ((1,), (1,)))
    unit_ref[...] = left_of(unit, 1)
    basis_ref[...] = unit * root


def factor_of(place, live, own, other, panel):
    rows, width = panel.shape
    return pl.pallas_call(
        factor_kernel,
        out_shape=(
            jax.ShapeDtypeStruct((width, 3 * width), BF16),
            jax.ShapeDtypeStruct((rows, 3 * width), BF16),
            struct(rows, width),
        ),
        in_specs=[SMEM, SMEM, VMEM, VMEM, VMEM],
        out_specs=(VMEM,) * 3,
        scratch_shapes=[pltpu.VMEM((width, width), F32)] * 2,
        cost_estimate=cost(6 * 10**9, 4 * rows * width),
        compiler_params=PARAMS,
        name="factor",
    )(place, live, own, other, panel)


def rest_kernel(other, place_ref, live_ref, inverse_ref, unit_ref, cross_ref, trail_ref, *refs):
    width = inverse_ref.shape[0]
    columns = trail_ref.shape[1]
    half = columns // 2
    core, chip, depth = place_of(place_ref)
    if other:
        top_before_ref, _, top_ref, rest_ref, top_scr, cross_scr, rest_scr, sem = refs
        side = 1 - core
    else:
        top_ref, rest_ref, top_scr, cross_scr, rest_scr, sem = refs
        side = core
    start = pl.multiple_of(side * half, half)
    part = width // PARTS
    for slot in range(SLOTS):
        lane = pl.multiple_of(jnp.bitwise_xor(chip, slot) * LANES, LANES)
        for piece in range(PARTS):
            row = pl.multiple_of(jnp.bitwise_xor(depth, piece) * part, 8)
            cross_scr[pl.ds(row, part), pl.ds(lane, LANES)] = cross_ref[
                slot, piece * part : (piece + 1) * part, :
            ]
    pieces = half // STRIP
    copies = []
    for piece in range(pieces):
        at = slice(piece * STRIP, (piece + 1) * STRIP)
        to = pl.ds(start + piece * STRIP, STRIP)
        top = dot(inverse_ref[...], right_of(cross_scr[:, at]))
        top_scr[:, at] = top
        rest_scr[:, at] = masked(trail_ref, live_ref, to) - dot(unit_ref[...], right_of(top))
        copies.append(pltpu.make_async_copy(rest_scr.at[:, at], rest_ref.at[:, to], sem.at[piece]))
        copies[piece].start()
    wide = top_ref.shape[1]
    begin = place_ref[0] % (columns // wide) * wide
    mine = top_scr[:, pl.ds(pl.multiple_of(begin % half, LANES), wide)]
    if other:
        top_ref[...] = jnp.where(begin // half == side, mine, top_before_ref[...])
    else:
        top_ref[...] = mine
    for copy in copies:
        copy.wait()


def rest_of(other, place, live, inverse, unit, cross, trail, wide, before):
    rows, columns = trail.shape
    width = inverse.shape[0]
    half = columns // 2
    return pl.pallas_call(
        functools.partial(rest_kernel, other),
        out_shape=(struct(width, wide), struct(rows, columns)),
        in_specs=[SMEM] * 2 + [VMEM] * 4 + ([VMEM, ANY] if other else []),
        out_specs=(VMEM, ANY),
        scratch_shapes=[
            pltpu.VMEM((width, half), F32),
            pltpu.VMEM((width, half), F32),
            pltpu.VMEM((rows, half), F32),
            pltpu.SemaphoreType.DMA((half // STRIP,)),
        ],
        input_output_aliases={7: 1} if other else {},
        cost_estimate=cost(12 * (rows + width) * width * half, 8 * rows * half),
        compiler_params=PARAMS,
        name="rest_other" if other else "rest_own",
    )(place, live, inverse, unit, cross, trail, *before)


def swap(x):
    return lax.ppermute(x, "core", [(0, 1), (1, 0)])


def send(x, axes, size, shift):
    return lax.ppermute(x, axes, [(i, i ^ shift) for i in range(size)])


def tree(parts):
    return (parts[0] + parts[1]) + (parts[2] + parts[3])


def body(panel, trailing, live_rows):
    width, columns = panel.shape[1], trailing.shape[1]
    flat, deep = ("y", "x"), "z"
    wide = columns // (lax.axis_size("x") * 2)
    place = lax.axis_index(AXES)[None]
    tall, part = width // SLOTS, width // PARTS

    theirs, ours = products_of(place, live_rows, panel, trailing)
    pair = ours + swap(theirs)
    slots = [pair[0]] + [send(pair[k], flat, SLOTS, k) for k in range(1, SLOTS)]
    summed = tree(slots)
    gram = summed[:tall]
    pieces = [
        jnp.concatenate([gram, summed[tall + j * part : tall + (j + 1) * part]])
        for j in range(PARTS)
    ]
    pieces = [pieces[0]] + [send(pieces[j], deep, PARTS, j) for j in range(1, PARTS)]
    summed = tree(pieces)
    if lax.axis_size("far") > 1:
        summed = lax.psum(summed, "far")
    gram, cross = summed[:tall], summed[tall:]
    gram_own = jnp.stack([gram] + [send(gram, flat, SLOTS, k) for k in range(1, SLOTS)])
    cross = jnp.concatenate([cross] + [send(cross, deep, PARTS, j) for j in range(1, PARTS)])
    cross_own = [cross] + [send(cross, flat, SLOTS, k) for k in range(1, SLOTS)]
    inverse, unit, basis = factor_of(place, live_rows, gram_own, swap(gram_own), panel)
    *cross_own, inverse = lax.optimization_barrier((*cross_own, inverse))
    cross_own = jnp.stack(cross_own)
    cross_other = swap(cross_own)
    args = (place, live_rows, inverse, unit)
    before = rest_of(False, *args, cross_own, trailing, wide, ())
    top, rest = rest_of(True, *args, cross_other, trailing, wide, before)
    return basis, top, rest


def solution(mesh):
    rows, subs = mesh.shape["rows"], mesh.shape["sub"]
    grid = Mesh(mesh.devices.reshape(rows // (2 * PARTS), PARTS, 2, subs // 2, 2), AXES)
    in_specs = (P(AXES, None), P(AXES, None), P(AXES))
    out_specs = (P(AXES, None), P(None, ("x", "core")), P(AXES, None))
    return jax.shard_map(
        body, mesh=grid, in_specs=in_specs, out_specs=out_specs, check_vma=False
    )
```

```python
import functools

import jax
import jax.numpy as jnp
from jax import lax
from jax.experimental import pallas as pl
from jax.experimental.pallas import tpu as pltpu
from jax.sharding import Mesh
from jax.sharding import PartitionSpec as P

AXES = ("far", "z", "y", "x", "core")
SLOTS = 4
PARTS = 4
F32 = jnp.float32
BF16 = jnp.bfloat16
LANES = 128
BLOCK = 32
BATCH = 16
STRIP = 512
EXTRA = 8
SMEM = pl.BlockSpec(memory_space=pltpu.SMEM)
VMEM = pl.BlockSpec(memory_space=pltpu.VMEM)
ANY = pl.BlockSpec(memory_space=pl.ANY)
HBM = pl.BlockSpec(memory_space=pltpu.HBM)
PARAMS = pltpu.CompilerParams(vmem_limit_bytes=16 << 20)


def in_hbm(x):
    return pltpu.with_memory_space_constraint(x, pltpu.HBM)


def place_of(ref):
    number = ref[0]
    return number % 2, number // 2 % SLOTS, number // (2 * SLOTS) % PARTS


def parts_of(x):
    high = x.astype(BF16)
    rest = x - high.astype(F32)
    middle = rest.astype(BF16)
    return high, middle, (rest - middle.astype(F32)).astype(BF16)


def left_of(x, axis, count=3):
    a, b, c = parts_of(x)
    return jnp.concatenate([a, a, b, a, c, b][:count], axis=axis)


def right_of(x, count=3, axis=0):
    a, b, c = parts_of(x)
    return jnp.concatenate([a, b, a, c, a, b][:count], axis=axis)


def dot(left, right, contract=((1,), (0,))):
    return lax.dot_general(left, right, (contract, ((), ())), preferred_element_type=F32)


def masked(ref, live_ref, columns=slice(None)):
    rows = ref.shape[0]
    live = lax.broadcasted_iota(jnp.int32, (rows, 1), 0) < live_ref[0]
    return jnp.where(live, ref[:, columns], 0.0)


def struct(*shape):
    return jax.ShapeDtypeStruct(shape, F32)


def cost(flops, transferred):
    return pl.CostEstimate(flops=flops, bytes_accessed=transferred, transcendentals=0)


def place_products(place_ref, gram, cross, out_ref, cross_scr):
    width = cross.shape[0]
    _, chip, depth = place_of(place_ref)
    tall = LANES // SLOTS
    part = width // PARTS
    for tile in range(SLOTS):
        cross_scr[tile] = cross[:, tile * LANES : (tile + 1) * LANES]
    for slot in range(SLOTS):
        chunk = jnp.bitwise_xor(chip, slot)
        out_ref[slot, :tall, :] = gram[pl.ds(pl.multiple_of(chunk * tall, 8), tall), :]
        out_ref[slot, tall : tall + EXTRA, :] = gram[LANES:, :]
        for piece in range(PARTS):
            at = pl.multiple_of(jnp.bitwise_xor(depth, piece) * part, 8)
            to = tall + EXTRA + piece * part
            out_ref[slot, to : to + part, :] = cross_scr[chunk, pl.ds(at, part), :]


def triangle():
    shape = (LANES, LANES)
    row = lax.broadcasted_iota(jnp.int32, shape, 0)
    column = lax.broadcasted_iota(jnp.int32, shape, 1)
    return row, column


def pack_gram(gram, live, gram_ref):
    row, column = triangle()
    second = gram[LANES:, LANES:]
    gram_ref[0, :LANES, :] = gram[:LANES, LANES:]
    gram_ref[1, :LANES, :] = jnp.where(row <= column, gram[:LANES, :LANES], second)
    diagonal = jnp.sum(jnp.where(row == column, second, 0.0), axis=0, keepdims=True)
    count = jnp.full((EXTRA, LANES), live, jnp.int32).astype(F32)
    index = lax.broadcasted_iota(jnp.int32, (EXTRA, LANES), 0)
    for side in range(2):
        gram_ref[side, LANES:, :] = jnp.where(index == 0, diagonal, count)


def unpack_gram(packed_ref, gram_ref):
    row, column = triangle()
    packed = packed_ref[1, :LANES, :]
    turned = packed.T
    diagonal = packed_ref[1, LANES : LANES + 1, :]
    gram_ref[:LANES, :LANES] = jnp.where(row <= column, packed, turned)
    gram_ref[:LANES, LANES:] = packed_ref[0, :LANES, :]
    second = jnp.where(row > column, packed, turned)
    gram_ref[LANES:, LANES:] = jnp.where(row == column, diagonal, second)
    return packed_ref[1, LANES + 1 : LANES + 2, 0:1]


def other_kernel(
    place_ref, live_ref, panel_ref, trail_ref, out_ref, left_ref, gram_ref, half_ref,
    cross_scr, panel_scr, trail_scr, panel_sem, trail_sem, half_sem,
):
    columns = trail_ref.shape[1]
    core = place_of(place_ref)[0]
    wide = columns // 2

    def columns_of(side):
        return trail_ref.at[:, pl.ds(pl.multiple_of(side * wide, LANES), wide)]

    copy_panel = pltpu.make_async_copy(panel_ref, panel_scr, panel_sem)
    copy_trail = pltpu.make_async_copy(columns_of(1 - core), trail_scr, trail_sem)
    copy_half = pltpu.make_async_copy(columns_of(core), half_ref, half_sem)
    copy_panel.start()
    copy_trail.start()
    copy_half.start()
    copy_panel.wait()
    rows = panel_scr.shape[0]
    panel = masked(panel_scr, live_ref)
    left = left_of(panel.T, 1, 6)
    left_ref[...] = left[:, : 3 * rows]
    pack_gram(dot(left, right_of(panel, 6)), live_ref[0], gram_ref)
    copy_trail.wait()
    cross = dot(left[:, : 3 * rows], right_of(masked(trail_scr, live_ref)))
    place_products(place_ref, gram_ref.at[1 - core], cross, out_ref, cross_scr)
    copy_half.wait()


def own_kernel(place_ref, live_ref, left_ref, gram_ref, half_ref, out_ref, cross_scr):
    cross = dot(left_ref[...], right_of(masked(half_ref, live_ref)))
    core = place_of(place_ref)[0]
    place_products(place_ref, gram_ref.at[core], cross, out_ref, cross_scr)


def products_of(place, live, panel, trail):
    rows, width = panel.shape
    columns = trail.shape[1]
    out = struct(SLOTS, LANES // SLOTS + EXTRA + width, LANES)
    work = cost(6 * rows * width * columns // 2, 2 * rows * columns)
    cross_scr = pltpu.VMEM((SLOTS, width, LANES), F32)
    theirs, *handed = pl.pallas_call(
        other_kernel,
        out_shape=(
            out,
            jax.ShapeDtypeStruct((width, 3 * rows), BF16),
            struct(2, LANES + EXTRA, LANES),
            struct(rows, columns // 2),
        ),
        in_specs=[SMEM, SMEM, HBM, HBM],
        out_specs=(VMEM,) * 4,
        scratch_shapes=[
            cross_scr,
            pltpu.VMEM((rows, width), F32),
            pltpu.VMEM((rows, columns // 2), F32),
        ]
        + [pltpu.SemaphoreType.DMA] * 3,
        cost_estimate=work,
        compiler_params=PARAMS,
        name="products_other",
    )(place, live, in_hbm(panel), in_hbm(trail))
    ours = pl.pallas_call(
        own_kernel,
        out_shape=out,
        in_specs=[SMEM, SMEM] + [VMEM] * 3,
        out_specs=VMEM,
        scratch_shapes=[cross_scr],
        cost_estimate=work,
        compiler_params=PARAMS,
        name="products_own",
    )(place, live, *handed)
    return theirs, ours


def across(x, lane):
    return jnp.broadcast_to(x[:, lane : lane + 1], (8, LANES))


def down(x, row):
    return jnp.broadcast_to(x[row : row + 1, :], (8, LANES))


def eliminate(rows, first):
    groups = len(rows)
    index = lax.broadcasted_iota(jnp.int32, (8, LANES), 0)
    pivots = [jnp.ones((8, LANES), F32) for _ in range(groups)]
    for start in range(0, BLOCK, BATCH):
        columns = {
            (group, j): across(rows[group][0], first + j)
            for j in range(start, start + BATCH)
            for group in range(j // 8, groups)
        }
        for j in range(start, start + BATCH, 2):
            home, place = divmod(j, 8)
            a = down(columns[home, j], place)
            b = down(columns[home, j], place + 1)
            c = down(columns[home, j + 1], place + 1)
            minor = a * c - b * b
            over_a, over_minor = 1.0 / a, 1.0 / minor
            ratio = b * over_a
            pivots[home] = jnp.where(index == place, a, pivots[home])
            pivots[home] = jnp.where(index == place + 1, minor * over_a, pivots[home])
            first_factor, second_factor = {}, {}
            for group in range(home, groups):
                one = columns[group, j]
                two = columns[group, j + 1] * a - one * b
                if group == home:
                    one = jnp.where(index > place, one, 0.0)
                    two = jnp.where(index > place + 1, two, 0.0)
                first_factor[group] = one * over_a
                second_factor[group] = two * over_minor
            for m in range(j + 2, start + BATCH):
                value = down(columns[m // 8, j], m % 8)
                other = down(columns[m // 8, j + 1], m % 8) - ratio * value
                for group in range(m // 8, groups):
                    columns[group, m] = (
                        columns[group, m]
                        - first_factor[group] * value
                        - second_factor[group] * other
                    )
            for tile in range(len(rows[0])):
                value = down(rows[home][tile], place)
                other = down(rows[home][tile], place + 1) - ratio * value
                for group in first_factor:
                    rows[group][tile] = (
                        rows[group][tile]
                        - first_factor[group] * value
                        - second_factor[group] * other
                    )
    return pivots


def factor_inverse(gram_ref, inverse_ref):
    size = gram_ref.shape[0]
    row = lax.broadcasted_iota(jnp.int32, (size, size), 0)
    column = lax.broadcasted_iota(jnp.int32, (size, size), 1)
    inverse_ref[...] = jnp.where(row == column, 1.0, 0.0)
    tiles = size // LANES
    groups = BLOCK // 8

    def tile_of(index):
        return slice(index * LANES, (index + 1) * LANES)

    for start in range(0, size, BLOCK):
        stop = start + BLOCK
        here = start // LANES
        rows = []
        for group in range(groups):
            at = slice(start + 8 * group, start + 8 * group + 8)
            rows.append(
                [gram_ref[at, tile_of(t)] for t in range(here, tiles)]
                + [inverse_ref[at, tile_of(t)] for t in range(here + 1)]
            )
        pivots = eliminate(rows, start % LANES)
        for group in range(groups):
            scale = lax.rsqrt(pivots[group])
            rows[group] = [value * scale for value in rows[group]]
            at = slice(start + 8 * group, start + 8 * group + 8)
            for t in range(here + 1):
                inverse_ref[at, tile_of(t)] = rows[group][tiles - here + t]
        if stop == size:
            break
        base = stop // LANES
        stacked = [
            jnp.concatenate([rows[group][i] for group in range(groups)], axis=0)
            for i in range(base - here, len(rows[0]))
        ]
        left = jnp.concatenate(stacked[: tiles - base], axis=1)
        product = dot(
            left_of(left, 0, 6), right_of(jnp.concatenate(stacked, axis=1), 6), ((0,), (0,))
        )[stop - base * LANES :]
        for i, t in enumerate(range(base, tiles)):
            gram_ref[stop:, tile_of(t)] -= product[:, tile_of(i)]
        for t in range(here + 1):
            inverse_ref[stop:, tile_of(t)] -= product[:, tile_of(tiles - base + t)]


def factor_kernel(
    place_ref, live_ref, own_ref, other_ref, panel_ref, left_ref, unit_ref, basis_ref,
    gram_ref, inverse_ref, packed_ref,
):
    core, chip, _ = place_of(place_ref)
    tall = LANES // SLOTS
    for side, ref in ((core, own_ref), (1 - core, other_ref)):
        for slot in range(SLOTS):
            chunk = jnp.bitwise_xor(chip, slot)
            row = pl.multiple_of(chunk * tall, 8)
            packed_ref[side, pl.ds(row, tall), :] = ref[slot, :tall, :]

            @pl.when(chunk == 0)
            def _(side=side, ref=ref, slot=slot):
                packed_ref[side, LANES:, :] = ref[slot, tall:, :]

    root = jnp.sqrt(unpack_gram(packed_ref, gram_ref))
    factor_inverse(gram_ref, inverse_ref)
    inverse = inverse_ref[...]
    left_ref[...] = left_of(inverse, 1)
    unit = dot(left_of(masked(panel_ref, live_ref), 1), right_of(inverse, axis=1), ((1,), (1,)))
    unit_ref[...] = left_of(unit, 1)
    basis_ref[...] = unit * root


def factor_of(place, live, own, other, panel):
    rows, width = panel.shape
    return pl.pallas_call(
        factor_kernel,
        out_shape=(
            jax.ShapeDtypeStruct((width, 3 * width), BF16),
            jax.ShapeDtypeStruct((rows, 3 * width), BF16),
            struct(rows, width),
        ),
        in_specs=[SMEM, SMEM, VMEM, VMEM, VMEM],
        out_specs=(VMEM,) * 3,
        scratch_shapes=[pltpu.VMEM((width, width), F32)] * 2
        + [pltpu.VMEM((2, LANES + EXTRA, LANES), F32)],
        cost_estimate=cost(6 * 10**9, 4 * rows * width),
        compiler_params=PARAMS,
        name="factor",
    )(place, live, own, other, panel)


def rest_kernel(other, place_ref, live_ref, inverse_ref, unit_ref, cross_ref, trail_ref, *refs):
    width = inverse_ref.shape[0]
    columns = trail_ref.shape[1]
    half = columns // 2
    core, chip, depth = place_of(place_ref)
    if other:
        top_before_ref, _, top_ref, rest_ref, top_scr, cross_scr, rest_scr, sem = refs
        side = 1 - core
    else:
        top_ref, rest_ref, top_scr, cross_scr, rest_scr, sem = refs
        side = core
    start = pl.multiple_of(side * half, half)
    part = width // PARTS
    for slot in range(SLOTS):
        lane = pl.multiple_of(jnp.bitwise_xor(chip, slot) * LANES, LANES)
        for piece in range(PARTS):
            row = pl.multiple_of(jnp.bitwise_xor(depth, piece) * part, 8)
            cross_scr[pl.ds(row, part), pl.ds(lane, LANES)] = cross_ref[
                slot, piece * part : (piece + 1) * part, :
            ]
    pieces = half // STRIP
    copies = []
    for piece in range(pieces):
        at = slice(piece * STRIP, (piece + 1) * STRIP)
        to = pl.ds(start + piece * STRIP, STRIP)
        top = dot(inverse_ref[...], right_of(cross_scr[:, at]))
        top_scr[:, at] = top
        rest_scr[:, at] = masked(trail_ref, live_ref, to) - dot(unit_ref[...], right_of(top))
        copies.append(pltpu.make_async_copy(rest_scr.at[:, at], rest_ref.at[:, to], sem.at[piece]))
        copies[piece].start()
    wide = top_ref.shape[1]
    begin = place_ref[0] % (columns // wide) * wide
    mine = top_scr[:, pl.ds(pl.multiple_of(begin % half, LANES), wide)]
    if other:
        top_ref[...] = jnp.where(begin // half == side, mine, top_before_ref[...])
    else:
        top_ref[...] = mine
    for copy in copies:
        copy.wait()


def rest_of(other, place, live, inverse, unit, cross, trail, wide, before):
    rows, columns = trail.shape
    width = inverse.shape[0]
    half = columns // 2
    return pl.pallas_call(
        functools.partial(rest_kernel, other),
        out_shape=(struct(width, wide), struct(rows, columns)),
        in_specs=[SMEM] * 2 + [VMEM] * 4 + ([VMEM, ANY] if other else []),
        out_specs=(VMEM, ANY),
        scratch_shapes=[
            pltpu.VMEM((width, half), F32),
            pltpu.VMEM((width, half), F32),
            pltpu.VMEM((rows, half), F32),
            pltpu.SemaphoreType.DMA((half // STRIP,)),
        ],
        input_output_aliases={7: 1} if other else {},
        cost_estimate=cost(12 * (rows + width) * width * half, 8 * rows * half),
        compiler_params=PARAMS,
        name="rest_other" if other else "rest_own",
    )(place, live, inverse, unit, cross, trail, *before)


def swap(x):
    return lax.ppermute(x, "core", [(0, 1), (1, 0)])


def send(x, axes, size, shift):
    return lax.ppermute(x, axes, [(i, i ^ shift) for i in range(size)])


def tree(parts):
    return (parts[0] + parts[1]) + (parts[2] + parts[3])


def body(panel, trailing, live_rows):
    width, columns = panel.shape[1], trailing.shape[1]
    flat, deep = ("y", "x"), "z"
    wide = columns // (lax.axis_size("x") * 2)
    place = lax.axis_index(AXES)[None]
    tall, part = LANES // SLOTS + EXTRA, width // PARTS

    theirs, ours = products_of(place, live_rows, panel, trailing)
    pair = ours + swap(theirs)
    slots = [pair[0]] + [send(pair[k], flat, SLOTS, k) for k in range(1, SLOTS)]
    summed = tree(slots)
    gram = summed[:tall]
    pieces = [
        jnp.concatenate([gram, summed[tall + j * part : tall + (j + 1) * part]])
        for j in range(PARTS)
    ]
    pieces = [pieces[0]] + [send(pieces[j], deep, PARTS, j) for j in range(1, PARTS)]
    summed = tree(pieces)
    if lax.axis_size("far") > 1:
        summed = lax.psum(summed, "far")
    gram, cross = summed[:tall], summed[tall:]
    gram_own = jnp.stack([gram] + [send(gram, flat, SLOTS, k) for k in range(1, SLOTS)])
    cross = jnp.concatenate([cross] + [send(cross, deep, PARTS, j) for j in range(1, PARTS)])
    cross_own = [cross] + [send(cross, flat, SLOTS, k) for k in range(1, SLOTS)]
    inverse, unit, basis = factor_of(place, live_rows, gram_own, swap(gram_own), panel)
    *cross_own, inverse = lax.optimization_barrier((*cross_own, inverse))
    cross_own = jnp.stack(cross_own)
    cross_other = swap(cross_own)
    args = (place, live_rows, inverse, unit)
    before = rest_of(False, *args, cross_own, trailing, wide, ())
    top, rest = rest_of(True, *args, cross_other, trailing, wide, before)
    return basis, top, rest


def solution(mesh):
    rows, subs = mesh.shape["rows"], mesh.shape["sub"]
    grid = Mesh(mesh.devices.reshape(rows // (2 * PARTS), PARTS, 2, subs // 2, 2), AXES)
    in_specs = (P(AXES, None), P(AXES, None), P(AXES))
    out_specs = (P(AXES, None), P(None, ("x", "core")), P(AXES, None))
    return jax.shard_map(
        body, mesh=grid, in_specs=in_specs, out_specs=out_specs, check_vma=False
    )
```

```python
import functools

import jax
import jax.numpy as jnp
from jax import lax
from jax.experimental import pallas as pl
from jax.experimental.pallas import tpu as pltpu
from jax.sharding import Mesh
from jax.sharding import PartitionSpec as P

AXES = ("far", "z", "y", "x", "core")
SLOTS = 4
PARTS = 4
F32 = jnp.float32
BF16 = jnp.bfloat16
LANES = 128
BLOCK = 32
BATCH = 16
EXTRA = 8
SMEM = pl.BlockSpec(memory_space=pltpu.SMEM)
VMEM = pl.BlockSpec(memory_space=pltpu.VMEM)
ANY = pl.BlockSpec(memory_space=pl.ANY)
HBM = pl.BlockSpec(memory_space=pltpu.HBM)
PARAMS = pltpu.CompilerParams(vmem_limit_bytes=16 << 20)


def in_hbm(x):
    return pltpu.with_memory_space_constraint(x, pltpu.HBM)


def place_of(ref):
    number = ref[0]
    return number % 2, number // 2 % SLOTS, number // (2 * SLOTS) % PARTS


def parts_of(x):
    high = x.astype(BF16)
    rest = x - high.astype(F32)
    middle = rest.astype(BF16)
    return high, middle, (rest - middle.astype(F32)).astype(BF16)


def left_of(x, axis, count=3):
    a, b, c = parts_of(x)
    return jnp.concatenate([a, a, b, a, c, b][:count], axis=axis)


def right_of(x, count=3, axis=0):
    a, b, c = parts_of(x)
    return jnp.concatenate([a, b, a, c, a, b][:count], axis=axis)


def dot(left, right, contract=((1,), (0,))):
    return lax.dot_general(left, right, (contract, ((), ())), preferred_element_type=F32)


def masked(ref, live_ref, columns=slice(None)):
    rows = ref.shape[0]
    live = lax.broadcasted_iota(jnp.int32, (rows, 1), 0) < live_ref[0]
    return jnp.where(live, ref[:, columns], 0.0)


def struct(*shape):
    return jax.ShapeDtypeStruct(shape, F32)


def cost(flops, transferred):
    return pl.CostEstimate(flops=flops, bytes_accessed=transferred, transcendentals=0)


def place_products(place_ref, gram, cross, out_ref, cross_scr):
    width = cross.shape[0]
    _, chip, depth = place_of(place_ref)
    tall = LANES // SLOTS
    part = width // PARTS
    for tile in range(SLOTS):
        cross_scr[tile] = cross[:, tile * LANES : (tile + 1) * LANES]
    for slot in range(SLOTS):
        chunk = jnp.bitwise_xor(chip, slot)
        out_ref[slot, :tall, :] = gram[pl.ds(pl.multiple_of(chunk * tall, 8), tall), :]
        out_ref[slot, tall : tall + EXTRA, :] = gram[LANES:, :]
        for piece in range(PARTS):
            at = pl.multiple_of(jnp.bitwise_xor(depth, piece) * part, 8)
            to = tall + EXTRA + piece * part
            out_ref[slot, to : to + part, :] = cross_scr[chunk, pl.ds(at, part), :]


def triangle():
    shape = (LANES, LANES)
    row = lax.broadcasted_iota(jnp.int32, shape, 0)
    column = lax.broadcasted_iota(jnp.int32, shape, 1)
    return row, column


def pack_gram(gram, live, gram_ref):
    row, column = triangle()
    second = gram[LANES:, LANES:]
    gram_ref[0, :LANES, :] = gram[:LANES, LANES:]
    gram_ref[1, :LANES, :] = jnp.where(row <= column, gram[:LANES, :LANES], second)
    diagonal = jnp.sum(jnp.where(row == column, second, 0.0), axis=0, keepdims=True)
    count = jnp.full((EXTRA, LANES), live, jnp.int32).astype(F32)
    index = lax.broadcasted_iota(jnp.int32, (EXTRA, LANES), 0)
    for side in range(2):
        gram_ref[side, LANES:, :] = jnp.where(index == 0, diagonal, count)


def unpack_gram(packed_ref, gram_ref):
    row, column = triangle()
    packed = packed_ref[1, :LANES, :]
    turned = packed.T
    diagonal = packed_ref[1, LANES : LANES + 1, :]
    gram_ref[:LANES, :LANES] = jnp.where(row <= column, packed, turned)
    gram_ref[:LANES, LANES:] = packed_ref[0, :LANES, :]
    second = jnp.where(row > column, packed, turned)
    gram_ref[LANES:, LANES:] = jnp.where(row == column, diagonal, second)
    return packed_ref[1, LANES + 1 : LANES + 2, 0:1]


def other_kernel(
    place_ref, live_ref, panel_ref, trail_ref, out_ref, left_ref, gram_ref, half_ref, panel_scr,
    cross_scr, trail_scr, panel_sem, trail_sem, half_sem,
):
    columns = trail_ref.shape[1]
    core = place_of(place_ref)[0]
    wide = columns // 2

    def columns_of(side):
        return trail_ref.at[:, pl.ds(pl.multiple_of(side * wide, LANES), wide)]

    copy_panel = pltpu.make_async_copy(panel_ref, panel_scr, panel_sem)
    copy_trail = pltpu.make_async_copy(columns_of(1 - core), trail_scr, trail_sem)
    copy_half = pltpu.make_async_copy(columns_of(core), half_ref, half_sem)
    copy_panel.start()
    copy_trail.start()
    copy_half.start()
    copy_panel.wait()
    rows = panel_scr.shape[0]
    panel = masked(panel_scr, live_ref)
    left = left_of(panel.T, 1, 6)
    left_ref[...] = left[:, : 3 * rows]
    pack_gram(dot(left, right_of(panel, 6)), live_ref[0], gram_ref)
    copy_trail.wait()
    cross = dot(left[:, : 3 * rows], right_of(masked(trail_scr, live_ref)))
    place_products(place_ref, gram_ref.at[1 - core], cross, out_ref, cross_scr)
    copy_half.wait()


def own_kernel(
    place_ref, live_ref, left_ref, gram_ref, half_ref, panel_ref, out_ref, rows_ref, cross_scr
):
    cross = dot(left_ref[...], right_of(masked(half_ref, live_ref)))
    core = place_of(place_ref)[0]
    place_products(place_ref, gram_ref.at[core], cross, out_ref, cross_scr)
    rows_ref[...] = left_of(masked(panel_ref, live_ref), 1)


def products_of(place, live, panel, trail):
    rows, width = panel.shape
    columns = trail.shape[1]
    out = struct(SLOTS, LANES // SLOTS + EXTRA + width, LANES)
    work = cost(6 * rows * width * columns // 2, 2 * rows * columns)
    cross_scr = pltpu.VMEM((SLOTS, width, LANES), F32)
    theirs, *handed = pl.pallas_call(
        other_kernel,
        out_shape=(
            out,
            jax.ShapeDtypeStruct((width, 3 * rows), BF16),
            struct(2, LANES + EXTRA, LANES),
            struct(rows, columns // 2),
            struct(rows, width),
        ),
        in_specs=[SMEM, SMEM, HBM, HBM],
        out_specs=(VMEM,) * 5,
        scratch_shapes=[cross_scr, pltpu.VMEM((rows, columns // 2), F32)]
        + [pltpu.SemaphoreType.DMA] * 3,
        cost_estimate=work,
        compiler_params=PARAMS,
        name="products_other",
    )(place, live, in_hbm(panel), in_hbm(trail))
    ours, panel_rows = pl.pallas_call(
        own_kernel,
        out_shape=(out, jax.ShapeDtypeStruct((rows, 3 * width), BF16)),
        in_specs=[SMEM, SMEM] + [VMEM] * 4,
        out_specs=(VMEM,) * 2,
        scratch_shapes=[cross_scr],
        cost_estimate=work,
        compiler_params=PARAMS,
        name="products_own",
    )(place, live, *handed)
    return theirs, ours, panel_rows


def across(x, lane):
    return jnp.broadcast_to(x[:, lane : lane + 1], (8, LANES))


def down(x, row):
    return jnp.broadcast_to(x[row : row + 1, :], (8, LANES))


def eliminate(rows, first):
    groups = len(rows)
    index = lax.broadcasted_iota(jnp.int32, (8, LANES), 0)
    lanes = lax.broadcasted_iota(jnp.int32, (8, LANES), 1)
    pivots = [jnp.ones((8, LANES), F32) for _ in range(groups)]
    for start in range(0, BLOCK, BATCH):
        columns = {
            (group, j): across(rows[group][0], first + j)
            for j in range(start, start + BATCH)
            for group in range(j // 8, groups)
        }
        for group in range(groups):
            taken = (lanes >= first + start) & (lanes < first + start + BATCH)
            unit = jnp.where(lanes == index + (first + 8 * group), 1.0, 0.0)
            rows[group][0] = jnp.where(taken, unit, rows[group][0])
        for j in range(start, start + BATCH, 2):
            home, place = divmod(j, 8)
            a = down(columns[home, j], place)
            b = down(columns[home, j], place + 1)
            c = down(columns[home, j + 1], place + 1)
            minor = a * c - b * b
            over_a, over_minor = 1.0 / a, 1.0 / minor
            ratio = b * over_a
            pivots[home] = jnp.where(index == place, a, pivots[home])
            pivots[home] = jnp.where(index == place + 1, minor * over_a, pivots[home])
            first_factor, second_factor = {}, {}
            for group in range(home, groups):
                one = columns[group, j]
                two = columns[group, j + 1] * a - one * b
                if group == home:
                    one = jnp.where(index > place, one, 0.0)
                    two = jnp.where(index > place + 1, two, 0.0)
                first_factor[group] = one * over_a
                second_factor[group] = two * over_minor
            for m in range(j + 2, start + BATCH):
                value = down(columns[m // 8, j], m % 8)
                other = down(columns[m // 8, j + 1], m % 8) - ratio * value
                for group in range(m // 8, groups):
                    columns[group, m] = (
                        columns[group, m]
                        - first_factor[group] * value
                        - second_factor[group] * other
                    )
            for tile in range(len(rows[0])):
                value = down(rows[home][tile], place)
                other = down(rows[home][tile], place + 1) - ratio * value
                for group in first_factor:
                    rows[group][tile] = (
                        rows[group][tile]
                        - first_factor[group] * value
                        - second_factor[group] * other
                    )
    return pivots


def factor_inverse(gram_ref):
    size = gram_ref.shape[0]
    tiles = size // LANES
    groups = BLOCK // 8

    def tile_of(index):
        return slice(index * LANES, (index + 1) * LANES)

    for start in range(0, size, BLOCK):
        stop = start + BLOCK
        here = start // LANES
        order = [here] + [t for t in range(tiles) if t != here]
        rows = [
            [gram_ref[start + 8 * group : start + 8 * group + 8, tile_of(t)] for t in order]
            for group in range(groups)
        ]
        pivots = eliminate(rows, start % LANES)
        scaled = {t: [] for t in order}
        for group in range(groups):
            scale = lax.rsqrt(pivots[group])
            for t, value in zip(order, rows[group]):
                scaled[t].append(value * scale)
        stacked = [jnp.concatenate(scaled[t], axis=0) for t in range(tiles)]
        lanes = lax.broadcasted_iota(jnp.int32, (BLOCK, LANES), 1)
        done = jnp.where(lanes < stop - here * LANES, stacked[here], 0.0)
        for t in range(tiles):
            gram_ref[start:stop, tile_of(t)] = (
                stacked[t] if t < here else done if t == here else jnp.zeros_like(done)
            )
        if stop == size:
            break
        base = stop // LANES
        left = jnp.concatenate(stacked[base:], axis=1)
        product = dot(
            left_of(left, 0, 6), right_of(jnp.concatenate(stacked, axis=1), 6), ((0,), (0,))
        )[stop - base * LANES :]
        for t in range(tiles):
            before = gram_ref[stop:, tile_of(t)]
            if t == here:
                lanes = lax.broadcasted_iota(jnp.int32, before.shape, 1) + here * LANES
                before = jnp.where((lanes >= start) & (lanes < stop), 0.0, before)
            gram_ref[stop:, tile_of(t)] = before - product[:, tile_of(t)]


def factor_kernel(
    place_ref, own_ref, other_ref, rows_ref, left_ref, split_ref, unit_ref, root_ref,
    inverse_ref, packed_ref,
):
    core, chip, _ = place_of(place_ref)
    tall = LANES // SLOTS
    for side, ref in ((core, own_ref), (1 - core, other_ref)):
        for slot in range(SLOTS):
            chunk = jnp.bitwise_xor(chip, slot)
            row = pl.multiple_of(chunk * tall, 8)
            packed_ref[side, pl.ds(row, tall), :] = ref[slot, :tall, :]

            @pl.when(chunk == 0)
            def _(side=side, ref=ref, slot=slot):
                packed_ref[side, LANES:, :] = ref[slot, tall:, :]

    root = jnp.sqrt(unpack_gram(packed_ref, inverse_ref))
    root_ref[...] = jnp.broadcast_to(root, root_ref.shape)
    factor_inverse(inverse_ref)
    inverse = inverse_ref[...]
    left_ref[...] = left_of(inverse, 1)
    unit = dot(rows_ref[...], right_of(inverse, axis=1), ((1,), (1,)))
    split_ref[...] = left_of(unit, 1)
    unit_ref[...] = unit


def factor_of(place, own, other, panel_rows):
    rows = panel_rows.shape[0]
    width = panel_rows.shape[1] // 3
    return pl.pallas_call(
        factor_kernel,
        out_shape=(
            jax.ShapeDtypeStruct((width, 3 * width), BF16),
            jax.ShapeDtypeStruct((rows, 3 * width), BF16),
            struct(rows, width),
            struct(8, LANES),
        ),
        in_specs=[SMEM, VMEM, VMEM, VMEM],
        out_specs=(VMEM,) * 4,
        scratch_shapes=[
            pltpu.VMEM((width, width), F32),
            pltpu.VMEM((2, LANES + EXTRA, LANES), F32),
        ],
        cost_estimate=cost(6 * 10**9, 4 * rows * width),
        compiler_params=PARAMS,
        name="factor",
    )(place, own, other, panel_rows)


def rest_kernel(other, place_ref, live_ref, inverse_ref, split_ref, cross_ref, trail_ref, *refs):
    width = inverse_ref.shape[0]
    columns = trail_ref.shape[1]
    half = columns // 2
    core, chip, depth = place_of(place_ref)
    if other:
        *_, top_ref, rest_ref, top_scr, cross_scr, rest_scr, top_sem, rest_sem = refs
        side = 1 - core
    else:
        unit_ref, root_ref, *refs = refs
        top_ref, rest_ref, basis_ref, top_scr, cross_scr, rest_scr, top_sem, rest_sem, *refs = refs
        basis_scr, basis_sem = refs
        side = core
        basis_scr[...] = unit_ref[...] * root_ref[0:1, 0:1]
        copy_basis = pltpu.make_async_copy(basis_scr, basis_ref, basis_sem)
        copy_basis.start()
    start = pl.multiple_of(side * half, half)
    part = width // PARTS
    for slot in range(SLOTS):
        lane = pl.multiple_of(jnp.bitwise_xor(chip, slot) * LANES, LANES)
        for piece in range(PARTS):
            row = pl.multiple_of(jnp.bitwise_xor(depth, piece) * part, 8)
            cross_scr[pl.ds(row, part), pl.ds(lane, LANES)] = cross_ref[
                slot, piece * part : (piece + 1) * part, :
            ]
    top = dot(inverse_ref[...], right_of(cross_scr[...]))
    top_scr[...] = top
    wide = top_ref.shape[1]
    begin = place_ref[0] % (columns // wide) * wide
    mine = begin // half == side
    copy_top = pltpu.make_async_copy(
        top_scr.at[:, pl.ds(pl.multiple_of(begin % half, LANES), wide)], top_ref, top_sem
    )

    @pl.when(mine)
    def _():
        copy_top.start()

    rest_scr[...] = masked(trail_ref, live_ref, pl.ds(start, half)) - dot(
        split_ref[...], right_of(top)
    )
    copy_rest = pltpu.make_async_copy(rest_scr, rest_ref.at[:, pl.ds(start, half)], rest_sem)
    copy_rest.start()
    copy_rest.wait()

    @pl.when(mine)
    def _():
        copy_top.wait()

    if not other:
        copy_basis.wait()


def rest_of(other, place, live, inverse, split, cross, trail, wide, more):
    rows, columns = trail.shape
    width = inverse.shape[0]
    half = columns // 2
    basis = [] if other else [struct(rows, width)]
    return pl.pallas_call(
        functools.partial(rest_kernel, other),
        out_shape=[struct(width, wide), struct(rows, columns)] + basis,
        in_specs=[SMEM] * 2 + [VMEM] * 4 + [ANY if other else VMEM] * 2,
        out_specs=[ANY] * (2 + len(basis)),
        scratch_shapes=[
            pltpu.VMEM((width, half), F32),
            pltpu.VMEM((width, half), F32),
            pltpu.VMEM((rows, half), F32),
            pltpu.SemaphoreType.DMA,
            pltpu.SemaphoreType.DMA,
        ]
        + ([] if other else [pltpu.VMEM((rows, width), F32), pltpu.SemaphoreType.DMA]),
        input_output_aliases={6: 0, 7: 1} if other else {},
        cost_estimate=cost(6 * (rows + width) * width * half, 8 * rows * half),
        compiler_params=PARAMS,
        name="rest_other" if other else "rest_own",
    )(place, live, inverse, split, cross, trail, *more)


def swap(x):
    return lax.ppermute(x, "core", [(0, 1), (1, 0)])


def send(x, axes, size, shift):
    return lax.ppermute(x, axes, [(i, i ^ shift) for i in range(size)])


def tree(parts):
    return (parts[0] + parts[1]) + (parts[2] + parts[3])


def body(panel, trailing, live_rows):
    width, columns = panel.shape[1], trailing.shape[1]
    flat, deep = ("y", "x"), "z"
    wide = columns // (lax.axis_size("x") * 2)
    place = lax.axis_index(AXES)[None]
    tall, part = LANES // SLOTS + EXTRA, width // PARTS

    theirs, ours, panel_rows = products_of(place, live_rows, panel, trailing)
    pair = ours + swap(theirs)
    slots = [pair[0]] + [send(pair[k], flat, SLOTS, k) for k in range(1, SLOTS)]
    summed = tree(slots)
    gram = summed[:tall]
    pieces = [
        jnp.concatenate([gram, summed[tall + j * part : tall + (j + 1) * part]])
        for j in range(PARTS)
    ]
    pieces = [pieces[0]] + [send(pieces[j], deep, PARTS, j) for j in range(1, PARTS)]
    summed = tree(pieces)
    if lax.axis_size("far") > 1:
        summed = lax.psum(summed, "far")
    gram, cross = summed[:tall], summed[tall:]
    gram_own = jnp.stack([gram] + [send(gram, flat, SLOTS, k) for k in range(1, SLOTS)])
    cross = jnp.concatenate([cross] + [send(cross, deep, PARTS, j) for j in range(1, PARTS)])
    cross_own = [cross] + [send(cross, flat, SLOTS, k) for k in range(1, SLOTS)]
    inverse, split, unit, root = factor_of(place, gram_own, swap(gram_own), panel_rows)
    *cross_own, inverse = lax.optimization_barrier((*cross_own, inverse))
    cross_own = jnp.stack(cross_own)
    cross_other = swap(cross_own)
    args = (place, live_rows, inverse, split)
    top, rest, basis = rest_of(False, *args, cross_own, trailing, wide, (unit, root))
    top, rest = rest_of(True, *args, cross_other, trailing, wide, (top, rest))
    return basis, top, rest


def solution(mesh):
    rows, subs = mesh.shape["rows"], mesh.shape["sub"]
    grid = Mesh(mesh.devices.reshape(rows // (2 * PARTS), PARTS, 2, subs // 2, 2), AXES)
    in_specs = (P(AXES, None), P(AXES, None), P(AXES))
    out_specs = (P(AXES, None), P(None, ("x", "core")), P(AXES, None))
    return jax.shard_map(
        body, mesh=grid, in_specs=in_specs, out_specs=out_specs, check_vma=False
    )
```

```python
import functools

import jax
import jax.numpy as jnp
from jax import lax
from jax.experimental import pallas as pl
from jax.experimental.pallas import tpu as pltpu
from jax.sharding import Mesh
from jax.sharding import PartitionSpec as P

AXES = ("far", "z", "y", "x", "core")
SLOTS = 4
PARTS = 4
F32 = jnp.float32
BF16 = jnp.bfloat16
LANES = 128
BLOCK = 32
BATCH = 16
EXTRA = 8
SMEM = pl.BlockSpec(memory_space=pltpu.SMEM)
VMEM = pl.BlockSpec(memory_space=pltpu.VMEM)
ANY = pl.BlockSpec(memory_space=pl.ANY)
HBM = pl.BlockSpec(memory_space=pltpu.HBM)
PARAMS = pltpu.CompilerParams(vmem_limit_bytes=16 << 20)


def in_hbm(x):
    return pltpu.with_memory_space_constraint(x, pltpu.HBM)


def place_of(ref):
    number = ref[0]
    return number % 2, number // 2 % SLOTS, number // (2 * SLOTS) % PARTS


def parts_of(x):
    high = x.astype(BF16)
    rest = x - high.astype(F32)
    middle = rest.astype(BF16)
    return high, middle, (rest - middle.astype(F32)).astype(BF16)


def left_of(x, axis, count=3):
    a, b, c = parts_of(x)
    return jnp.concatenate([a, a, b, a, c, b][:count], axis=axis)


def right_of(x, count=3, axis=0):
    a, b, c = parts_of(x)
    return jnp.concatenate([a, b, a, c, a, b][:count], axis=axis)


def dot(left, right, contract=((1,), (0,))):
    return lax.dot_general(left, right, (contract, ((), ())), preferred_element_type=F32)


def masked(ref, live_ref, columns=slice(None)):
    rows = ref.shape[0]
    live = lax.broadcasted_iota(jnp.int32, (rows, 1), 0) < live_ref[0]
    return jnp.where(live, ref[:, columns], 0.0)


def struct(*shape):
    return jax.ShapeDtypeStruct(shape, F32)


def cost(flops, transferred):
    return pl.CostEstimate(flops=flops, bytes_accessed=transferred, transcendentals=0)


def place_products(place_ref, gram, cross, out_refs, cross_scr):
    width = cross.shape[0]
    _, chip, depth = place_of(place_ref)
    tall = LANES // SLOTS
    part = width // PARTS
    for tile in range(SLOTS):
        cross_scr[tile] = cross[:, tile * LANES : (tile + 1) * LANES]
    for slot in range(SLOTS):
        chunk = jnp.bitwise_xor(chip, slot)
        out_ref = out_refs[slot]
        out_ref[:tall, :] = gram[pl.ds(pl.multiple_of(chunk * tall, 8), tall), :]
        out_ref[tall : tall + EXTRA, :] = gram[LANES:, :]
        for piece in range(PARTS):
            at = pl.multiple_of(jnp.bitwise_xor(depth, piece) * part, 8)
            to = tall + EXTRA + piece * part
            out_ref[to : to + part, :] = cross_scr[chunk, pl.ds(at, part), :]


def triangle():
    shape = (LANES, LANES)
    row = lax.broadcasted_iota(jnp.int32, shape, 0)
    column = lax.broadcasted_iota(jnp.int32, shape, 1)
    return row, column


def pack_gram(gram, live, gram_ref):
    row, column = triangle()
    second = gram[LANES:, LANES:]
    gram_ref[0, :LANES, :] = gram[:LANES, LANES:]
    gram_ref[1, :LANES, :] = jnp.where(row <= column, gram[:LANES, :LANES], second)
    diagonal = jnp.sum(jnp.where(row == column, second, 0.0), axis=0, keepdims=True)
    count = jnp.full((EXTRA, LANES), live, jnp.int32).astype(F32)
    index = lax.broadcasted_iota(jnp.int32, (EXTRA, LANES), 0)
    for side in range(2):
        gram_ref[side, LANES:, :] = jnp.where(index == 0, diagonal, count)


def unpack_gram(packed_ref, gram_ref):
    row, column = triangle()
    packed = packed_ref[1, :LANES, :]
    turned = packed.T
    diagonal = packed_ref[1, LANES : LANES + 1, :]
    gram_ref[:LANES, :LANES] = jnp.where(row <= column, packed, turned)
    gram_ref[:LANES, LANES:] = packed_ref[0, :LANES, :]
    second = jnp.where(row > column, packed, turned)
    gram_ref[LANES:, LANES:] = jnp.where(row == column, diagonal, second)
    return packed_ref[1, LANES + 1 : LANES + 2, 0:1]


def other_kernel(
    place_ref, live_ref, panel_ref, trail_ref, *refs
):
    out_refs = refs[:SLOTS]
    left_ref, gram_ref, half_ref, panel_scr, cross_scr, trail_scr, *sems = refs[SLOTS:]
    panel_sem, trail_sem, half_sem = sems
    columns = trail_ref.shape[1]
    core = place_of(place_ref)[0]
    wide = columns // 2

    def columns_of(side):
        return trail_ref.at[:, pl.ds(pl.multiple_of(side * wide, LANES), wide)]

    copy_panel = pltpu.make_async_copy(panel_ref, panel_scr, panel_sem)
    copy_trail = pltpu.make_async_copy(columns_of(1 - core), trail_scr, trail_sem)
    copy_half = pltpu.make_async_copy(columns_of(core), half_ref, half_sem)
    copy_panel.start()
    copy_trail.start()
    copy_half.start()
    copy_panel.wait()
    rows = panel_scr.shape[0]
    panel = masked(panel_scr, live_ref)
    left = left_of(panel.T, 1)
    left_ref[...] = left
    high, middle, low = parts_of(panel)
    mixed = dot(left[:, : 2 * rows], jnp.concatenate([middle, low], axis=0))
    gram = dot(left[:, rows:], jnp.concatenate([high, middle], axis=0)) + (mixed + mixed.T)
    pack_gram(gram, live_ref[0], gram_ref)
    copy_trail.wait()
    cross = dot(left, right_of(masked(trail_scr, live_ref)))
    place_products(place_ref, gram_ref.at[1 - core], cross, out_refs, cross_scr)
    copy_half.wait()


def own_kernel(
    place_ref, live_ref, left_ref, gram_ref, half_ref, panel_ref, *refs
):
    *out_refs, rows_ref, cross_scr = refs
    cross = dot(left_ref[...], right_of(masked(half_ref, live_ref)))
    core = place_of(place_ref)[0]
    place_products(place_ref, gram_ref.at[core], cross, out_refs, cross_scr)
    rows_ref[...] = left_of(masked(panel_ref, live_ref), 1)


def products_of(place, live, panel, trail):
    rows, width = panel.shape
    columns = trail.shape[1]
    out = (struct(LANES // SLOTS + EXTRA + width, LANES),) * SLOTS
    work = cost(6 * rows * width * columns // 2, 2 * rows * columns)
    cross_scr = pltpu.VMEM((SLOTS, width, LANES), F32)
    outs = pl.pallas_call(
        other_kernel,
        out_shape=(
            *out,
            jax.ShapeDtypeStruct((width, 3 * rows), BF16),
            struct(2, LANES + EXTRA, LANES),
            struct(rows, columns // 2),
            struct(rows, width),
        ),
        in_specs=[SMEM, SMEM, HBM, HBM],
        out_specs=(VMEM,) * (SLOTS + 4),
        scratch_shapes=[cross_scr, pltpu.VMEM((rows, columns // 2), F32)]
        + [pltpu.SemaphoreType.DMA] * 3,
        cost_estimate=work,
        compiler_params=PARAMS,
        name="products_other",
    )(place, live, in_hbm(panel), in_hbm(trail))
    theirs, handed = outs[:SLOTS], outs[SLOTS:]
    *ours, panel_rows = pl.pallas_call(
        own_kernel,
        out_shape=(*out, jax.ShapeDtypeStruct((rows, 3 * width), BF16)),
        in_specs=[SMEM, SMEM] + [VMEM] * 4,
        out_specs=(VMEM,) * (SLOTS + 1),
        scratch_shapes=[cross_scr],
        cost_estimate=work,
        compiler_params=PARAMS,
        name="products_own",
    )(place, live, *handed)
    return theirs, ours, panel_rows


def across(x, lane):
    return jnp.broadcast_to(x[:, lane : lane + 1], (8, LANES))


def down(x, row):
    return jnp.broadcast_to(x[row : row + 1, :], (8, LANES))


def eliminate(rows, first):
    groups = len(rows)
    index = lax.broadcasted_iota(jnp.int32, (8, LANES), 0)
    lanes = lax.broadcasted_iota(jnp.int32, (8, LANES), 1)
    pivots = [jnp.ones((8, LANES), F32) for _ in range(groups)]
    for start in range(0, BLOCK, BATCH):
        columns = {
            (group, j): across(rows[group][0], first + j)
            for j in range(start, start + BATCH)
            for group in range(j // 8, groups)
        }
        for group in range(groups):
            taken = (lanes >= first + start) & (lanes < first + start + BATCH)
            unit = jnp.where(lanes == index + (first + 8 * group), 1.0, 0.0)
            rows[group][0] = jnp.where(taken, unit, rows[group][0])
        for j in range(start, start + BATCH, 2):
            home, place = divmod(j, 8)
            a = down(columns[home, j], place)
            b = down(columns[home, j], place + 1)
            c = down(columns[home, j + 1], place + 1)
            minor = a * c - b * b
            over_a, over_minor = 1.0 / a, 1.0 / minor
            ratio = b * over_a
            pivots[home] = jnp.where(index == place, a, pivots[home])
            pivots[home] = jnp.where(index == place + 1, minor * over_a, pivots[home])
            first_factor, second_factor = {}, {}
            for group in range(home, groups):
                one = columns[group, j]
                two = columns[group, j + 1] * a - one * b
                if group == home:
                    one = jnp.where(index > place, one, 0.0)
                    two = jnp.where(index > place + 1, two, 0.0)
                first_factor[group] = one * over_a
                second_factor[group] = two * over_minor
            for m in range(j + 2, start + BATCH):
                value = down(columns[m // 8, j], m % 8)
                other = down(columns[m // 8, j + 1], m % 8) - ratio * value
                for group in range(m // 8, groups):
                    columns[group, m] = (
                        columns[group, m]
                        - first_factor[group] * value
                        - second_factor[group] * other
                    )
            for tile in range(len(rows[0])):
                value = down(rows[home][tile], place)
                other = down(rows[home][tile], place + 1) - ratio * value
                for group in first_factor:
                    rows[group][tile] = (
                        rows[group][tile]
                        - first_factor[group] * value
                        - second_factor[group] * other
                    )
    return pivots


def factor_inverse(gram_ref):
    size = gram_ref.shape[0]
    tiles = size // LANES
    groups = BLOCK // 8

    def tile_of(index):
        return slice(index * LANES, (index + 1) * LANES)

    for start in range(0, size, BLOCK):
        stop = start + BLOCK
        here = start // LANES
        order = [here] + [t for t in range(tiles) if t != here]
        rows = [
            [gram_ref[start + 8 * group : start + 8 * group + 8, tile_of(t)] for t in order]
            for group in range(groups)
        ]
        pivots = eliminate(rows, start % LANES)
        scaled = {t: [] for t in order}
        for group in range(groups):
            scale = lax.rsqrt(pivots[group])
            for t, value in zip(order, rows[group]):
                scaled[t].append(value * scale)
        stacked = [jnp.concatenate(scaled[t], axis=0) for t in range(tiles)]
        lanes = lax.broadcasted_iota(jnp.int32, (BLOCK, LANES), 1)
        done = jnp.where(lanes < stop - here * LANES, stacked[here], 0.0)
        for t in range(tiles):
            gram_ref[start:stop, tile_of(t)] = (
                stacked[t] if t < here else done if t == here else jnp.zeros_like(done)
            )
        if stop == size:
            break
        base = stop // LANES
        left = jnp.concatenate(stacked[base:], axis=1)
        product = dot(
            left_of(left, 0, 6), right_of(jnp.concatenate(stacked, axis=1), 6), ((0,), (0,))
        )[stop - base * LANES :]
        for t in range(tiles):
            before = gram_ref[stop:, tile_of(t)]
            if t == here:
                lanes = lax.broadcasted_iota(jnp.int32, before.shape, 1) + here * LANES
                before = jnp.where((lanes >= start) & (lanes < stop), 0.0, before)
            gram_ref[stop:, tile_of(t)] = before - product[:, tile_of(t)]


def factor_kernel(
    place_ref, own_ref, other_ref, rows_ref, left_ref, split_ref, unit_ref, root_ref,
    inverse_ref, packed_ref,
):
    core, chip, _ = place_of(place_ref)
    tall = LANES // SLOTS
    for side, ref in ((core, own_ref), (1 - core, other_ref)):
        for slot in range(SLOTS):
            chunk = jnp.bitwise_xor(chip, slot)
            row = pl.multiple_of(chunk * tall, 8)
            packed_ref[side, pl.ds(row, tall), :] = ref[slot, :tall, :]

            @pl.when(chunk == 0)
            def _(side=side, ref=ref, slot=slot):
                packed_ref[side, LANES:, :] = ref[slot, tall:, :]

    root = jnp.sqrt(unpack_gram(packed_ref, inverse_ref))
    root_ref[...] = jnp.broadcast_to(root, root_ref.shape)
    factor_inverse(inverse_ref)
    inverse = inverse_ref[...]
    left_ref[...] = left_of(inverse, 1)
    unit = dot(rows_ref[...], right_of(inverse, axis=1), ((1,), (1,)))
    split_ref[...] = left_of(unit, 1)
    unit_ref[...] = unit


def factor_of(place, own, other, panel_rows):
    rows = panel_rows.shape[0]
    width = panel_rows.shape[1] // 3
    return pl.pallas_call(
        factor_kernel,
        out_shape=(
            jax.ShapeDtypeStruct((width, 3 * width), BF16),
            jax.ShapeDtypeStruct((rows, 3 * width), BF16),
            struct(rows, width),
            struct(8, LANES),
        ),
        in_specs=[SMEM, VMEM, VMEM, VMEM],
        out_specs=(VMEM,) * 4,
        scratch_shapes=[
            pltpu.VMEM((width, width), F32),
            pltpu.VMEM((2, LANES + EXTRA, LANES), F32),
        ],
        cost_estimate=cost(6 * 10**9, 4 * rows * width),
        compiler_params=PARAMS,
        name="factor",
    )(place, own, other, panel_rows)


def rest_kernel(other, place_ref, live_ref, inverse_ref, split_ref, cross_ref, trail_ref, *refs):
    width = inverse_ref.shape[0]
    columns = trail_ref.shape[1]
    half = columns // 2
    core, chip, depth = place_of(place_ref)
    if other:
        *_, top_ref, rest_ref, top_scr, cross_scr, rest_scr, top_sem, rest_sem = refs
        side = 1 - core
    else:
        unit_ref, root_ref, *refs = refs
        top_ref, rest_ref, basis_ref, top_scr, cross_scr, rest_scr, top_sem, rest_sem, *refs = refs
        basis_scr, basis_sem = refs
        side = core
        basis_scr[...] = unit_ref[...] * root_ref[0:1, 0:1]
        copy_basis = pltpu.make_async_copy(basis_scr, basis_ref, basis_sem)
        copy_basis.start()
    start = pl.multiple_of(side * half, half)
    part = width // PARTS
    for slot in range(SLOTS):
        lane = pl.multiple_of(jnp.bitwise_xor(chip, slot) * LANES, LANES)
        for piece in range(PARTS):
            row = pl.multiple_of(jnp.bitwise_xor(depth, piece) * part, 8)
            cross_scr[pl.ds(row, part), pl.ds(lane, LANES)] = cross_ref[
                slot, piece * part : (piece + 1) * part, :
            ]
    top = dot(inverse_ref[...], right_of(cross_scr[...]))
    top_scr[...] = top
    wide = top_ref.shape[1]
    begin = place_ref[0] % (columns // wide) * wide
    mine = begin // half == side
    copy_top = pltpu.make_async_copy(
        top_scr.at[:, pl.ds(pl.multiple_of(begin % half, LANES), wide)], top_ref, top_sem
    )

    @pl.when(mine)
    def _():
        copy_top.start()

    rest_scr[...] = masked(trail_ref, live_ref, pl.ds(start, half)) - dot(
        split_ref[...], right_of(top)
    )
    copy_rest = pltpu.make_async_copy(rest_scr, rest_ref.at[:, pl.ds(start, half)], rest_sem)
    copy_rest.start()
    copy_rest.wait()

    @pl.when(mine)
    def _():
        copy_top.wait()

    if not other:
        copy_basis.wait()


def rest_of(other, place, live, inverse, split, cross, trail, wide, more):
    rows, columns = trail.shape
    width = inverse.shape[0]
    half = columns // 2
    basis = [] if other else [struct(rows, width)]
    return pl.pallas_call(
        functools.partial(rest_kernel, other),
        out_shape=[struct(width, wide), struct(rows, columns)] + basis,
        in_specs=[SMEM] * 2 + [VMEM] * 4 + [ANY if other else VMEM] * 2,
        out_specs=[ANY] * (2 + len(basis)),
        scratch_shapes=[
            pltpu.VMEM((width, half), F32),
            pltpu.VMEM((width, half), F32),
            pltpu.VMEM((rows, half), F32),
            pltpu.SemaphoreType.DMA,
            pltpu.SemaphoreType.DMA,
        ]
        + ([] if other else [pltpu.VMEM((rows, width), F32), pltpu.SemaphoreType.DMA]),
        input_output_aliases={6: 0, 7: 1} if other else {},
        cost_estimate=cost(6 * (rows + width) * width * half, 8 * rows * half),
        compiler_params=PARAMS,
        name="rest_other" if other else "rest_own",
    )(place, live, inverse, split, cross, trail, *more)


def swap(x):
    return lax.ppermute(x, "core", [(0, 1), (1, 0)])


def send(x, axes, size, shift):
    return lax.ppermute(x, axes, [(i, i ^ shift) for i in range(size)])


def tree(parts):
    return (parts[0] + parts[1]) + (parts[2] + parts[3])


def body(panel, trailing, live_rows):
    width, columns = panel.shape[1], trailing.shape[1]
    flat, deep = ("y", "x"), "z"
    wide = columns // (lax.axis_size("x") * 2)
    place = lax.axis_index(AXES)[None]
    tall, part = LANES // SLOTS + EXTRA, width // PARTS

    theirs, ours, panel_rows = products_of(place, live_rows, panel, trailing)
    order = [3, 1, 2, 0]
    arrived = {k: swap(theirs[k]) for k in order}
    pair = {k: ours[k] + arrived[k] for k in order}
    slots = [pair[0]] + [send(pair[k], flat, SLOTS, k) for k in range(1, SLOTS)]
    summed = tree(slots)
    gram = summed[:tall]
    pieces = [
        jnp.concatenate([gram, summed[tall + j * part : tall + (j + 1) * part]])
        for j in range(PARTS)
    ]
    pieces = [pieces[0]] + [send(pieces[j], deep, PARTS, j) for j in range(1, PARTS)]
    summed = tree(pieces)
    if lax.axis_size("far") > 1:
        summed = lax.psum(summed, "far")
    gram, cross = summed[:tall], summed[tall:]
    gram_own = jnp.stack([gram] + [send(gram, flat, SLOTS, k) for k in range(1, SLOTS)])
    cross = jnp.concatenate([cross] + [send(cross, deep, PARTS, j) for j in range(1, PARTS)])
    cross_own = [cross] + [send(cross, flat, SLOTS, k) for k in range(1, SLOTS)]
    inverse, split, unit, root = factor_of(place, gram_own, swap(gram_own), panel_rows)
    *cross_own, inverse = lax.optimization_barrier((*cross_own, inverse))
    cross_own = jnp.stack(cross_own)
    cross_other = swap(cross_own)
    args = (place, live_rows, inverse, split)
    top, rest, basis = rest_of(False, *args, cross_own, trailing, wide, (unit, root))
    top, rest = rest_of(True, *args, cross_other, trailing, wide, (top, rest))
    return basis, top, rest


def solution(mesh):
    rows, subs = mesh.shape["rows"], mesh.shape["sub"]
    grid = Mesh(mesh.devices.reshape(rows // (2 * PARTS), PARTS, 2, subs // 2, 2), AXES)
    in_specs = (P(AXES, None), P(AXES, None), P(AXES))
    out_specs = (P(AXES, None), P(None, ("x", "core")), P(AXES, None))
    return jax.shard_map(
        body, mesh=grid, in_specs=in_specs, out_specs=out_specs, check_vma=False
    )
```

```python
import functools

import jax
import jax.numpy as jnp
from jax import lax
from jax.experimental import pallas as pl
from jax.experimental.pallas import tpu as pltpu
from jax.sharding import Mesh
from jax.sharding import PartitionSpec as P

AXES = ("far", "z", "y", "x", "core")
SLOTS = 4
PARTS = 4
F32 = jnp.float32
BF16 = jnp.bfloat16
LANES = 128
BLOCK = 32
BATCH = 16
EXTRA = 8
SMEM = pl.BlockSpec(memory_space=pltpu.SMEM)
VMEM = pl.BlockSpec(memory_space=pltpu.VMEM)
ANY = pl.BlockSpec(memory_space=pl.ANY)
HBM = pl.BlockSpec(memory_space=pltpu.HBM)
PARAMS = pltpu.CompilerParams(vmem_limit_bytes=16 << 20)


def in_hbm(x):
    return pltpu.with_memory_space_constraint(x, pltpu.HBM)


def place_of(ref):
    number = ref[0]
    return number % 2, number // 2 % SLOTS, number // (2 * SLOTS) % PARTS


def parts_of(x):
    high = x.astype(BF16)
    rest = x - high.astype(F32)
    middle = rest.astype(BF16)
    return high, middle, (rest - middle.astype(F32)).astype(BF16)


def left_of(x, axis, count=3):
    a, b, c = parts_of(x)
    return jnp.concatenate([a, a, b, a, c, b][:count], axis=axis)


def right_of(x, count=3, axis=0):
    a, b, c = parts_of(x)
    return jnp.concatenate([a, b, a, c, a, b][:count], axis=axis)


def dot(left, right, contract=((1,), (0,))):
    return lax.dot_general(left, right, (contract, ((), ())), preferred_element_type=F32)


def masked(ref, live_ref, columns=slice(None)):
    rows = ref.shape[0]
    live = lax.broadcasted_iota(jnp.int32, (rows, 1), 0) < live_ref[0]
    return jnp.where(live, ref[:, columns], 0.0)


def struct(*shape):
    return jax.ShapeDtypeStruct(shape, F32)


def cost(flops, transferred):
    return pl.CostEstimate(flops=flops, bytes_accessed=transferred, transcendentals=0)


def place_products(place_ref, gram, cross, out_refs, cross_scr):
    width = cross.shape[0]
    _, chip, depth = place_of(place_ref)
    tall = LANES // SLOTS
    part = width // PARTS
    for tile in range(SLOTS):
        cross_scr[tile] = cross[:, tile * LANES : (tile + 1) * LANES]
    for slot in range(SLOTS):
        chunk = jnp.bitwise_xor(chip, slot)
        out_ref = out_refs[slot]
        out_ref[:tall, :] = gram[pl.ds(pl.multiple_of(chunk * tall, 8), tall), :]
        out_ref[tall : tall + EXTRA, :] = gram[LANES:, :]
        for piece in range(PARTS):
            at = pl.multiple_of(jnp.bitwise_xor(depth, piece) * part, 8)
            to = tall + EXTRA + piece * part
            out_ref[to : to + part, :] = cross_scr[chunk, pl.ds(at, part), :]


def triangle():
    shape = (LANES, LANES)
    row = lax.broadcasted_iota(jnp.int32, shape, 0)
    column = lax.broadcasted_iota(jnp.int32, shape, 1)
    return row, column


def pack_gram(gram, live, gram_ref):
    row, column = triangle()
    second = gram[LANES:, LANES:]
    gram_ref[0, :LANES, :] = gram[:LANES, LANES:]
    gram_ref[1, :LANES, :] = jnp.where(row <= column, gram[:LANES, :LANES], second)
    diagonal = jnp.sum(jnp.where(row == column, second, 0.0), axis=0, keepdims=True)
    count = jnp.full((EXTRA, LANES), live, jnp.int32).astype(F32)
    index = lax.broadcasted_iota(jnp.int32, (EXTRA, LANES), 0)
    for side in range(2):
        gram_ref[side, LANES:, :] = jnp.where(index == 0, diagonal, count)


def unpack_gram(packed_ref, gram_ref):
    row, column = triangle()
    packed = packed_ref[1, :LANES, :]
    turned = packed.T
    diagonal = packed_ref[1, LANES : LANES + 1, :]
    gram_ref[:LANES, :LANES] = jnp.where(row <= column, packed, turned)
    gram_ref[:LANES, LANES:] = packed_ref[0, :LANES, :]
    second = jnp.where(row > column, packed, turned)
    gram_ref[LANES:, LANES:] = jnp.where(row == column, diagonal, second)
    return packed_ref[1, LANES + 1 : LANES + 2, 0:1]


def other_kernel(
    place_ref, live_ref, panel_ref, trail_ref, *refs
):
    out_refs = refs[:SLOTS]
    left_ref, gram_ref, half_ref, panel_scr, cross_scr, trail_scr, *sems = refs[SLOTS:]
    panel_sem, trail_sem, half_sem = sems
    columns = trail_ref.shape[1]
    core = place_of(place_ref)[0]
    wide = columns // 2

    def columns_of(side):
        return trail_ref.at[:, pl.ds(pl.multiple_of(side * wide, LANES), wide)]

    copy_panel = pltpu.make_async_copy(panel_ref, panel_scr, panel_sem)
    copy_trail = pltpu.make_async_copy(columns_of(1 - core), trail_scr, trail_sem)
    copy_half = pltpu.make_async_copy(columns_of(core), half_ref, half_sem)
    copy_panel.start()
    copy_trail.start()
    copy_half.start()
    copy_panel.wait()
    rows = panel_scr.shape[0]
    panel = masked(panel_scr, live_ref)
    left = left_of(panel.T, 1)
    left_ref[...] = left
    high, middle, low = parts_of(panel)
    mixed = dot(left[:, : 2 * rows], jnp.concatenate([middle, low], axis=0))
    gram = dot(left[:, rows:], jnp.concatenate([high, middle], axis=0)) + (mixed + mixed.T)
    pack_gram(gram, live_ref[0], gram_ref)
    copy_trail.wait()
    cross = dot(left, right_of(masked(trail_scr, live_ref)))
    place_products(place_ref, gram_ref.at[1 - core], cross, out_refs, cross_scr)
    copy_half.wait()


def own_kernel(
    place_ref, live_ref, left_ref, gram_ref, half_ref, panel_ref, *refs
):
    *out_refs, rows_ref, cross_scr = refs
    cross = dot(left_ref[...], right_of(masked(half_ref, live_ref)))
    core = place_of(place_ref)[0]
    place_products(place_ref, gram_ref.at[core], cross, out_refs, cross_scr)
    rows_ref[...] = left_of(masked(panel_ref, live_ref), 1)


def products_of(place, live, panel, trail):
    rows, width = panel.shape
    columns = trail.shape[1]
    out = (struct(LANES // SLOTS + EXTRA + width, LANES),) * SLOTS
    work = cost(6 * rows * width * columns // 2, 2 * rows * columns)
    cross_scr = pltpu.VMEM((SLOTS, width, LANES), F32)
    outs = pl.pallas_call(
        other_kernel,
        out_shape=(
            *out,
            jax.ShapeDtypeStruct((width, 3 * rows), BF16),
            struct(2, LANES + EXTRA, LANES),
            struct(rows, columns // 2),
            struct(rows, width),
        ),
        in_specs=[SMEM, SMEM, HBM, HBM],
        out_specs=(VMEM,) * (SLOTS + 4),
        scratch_shapes=[cross_scr, pltpu.VMEM((rows, columns // 2), F32)]
        + [pltpu.SemaphoreType.DMA] * 3,
        cost_estimate=work,
        compiler_params=PARAMS,
        name="products_other",
    )(place, live, in_hbm(panel), in_hbm(trail))
    theirs, handed = outs[:SLOTS], outs[SLOTS:]
    *ours, panel_rows = pl.pallas_call(
        own_kernel,
        out_shape=(*out, jax.ShapeDtypeStruct((rows, 3 * width), BF16)),
        in_specs=[SMEM, SMEM] + [VMEM] * 4,
        out_specs=(VMEM,) * (SLOTS + 1),
        scratch_shapes=[cross_scr],
        cost_estimate=work,
        compiler_params=PARAMS,
        name="products_own",
    )(place, live, *handed)
    return theirs, ours, panel_rows


def across(x, lane):
    return jnp.broadcast_to(x[:, lane : lane + 1], (8, LANES))


def down(x, row):
    return jnp.broadcast_to(x[row : row + 1, :], (8, LANES))


def eliminate(rows, first):
    groups = len(rows)
    index = lax.broadcasted_iota(jnp.int32, (8, LANES), 0)
    lanes = lax.broadcasted_iota(jnp.int32, (8, LANES), 1)
    pivots = [jnp.ones((8, LANES), F32) for _ in range(groups)]
    for start in range(0, BLOCK, BATCH):
        columns = {
            (group, j): across(rows[group][0], first + j)
            for j in range(start, start + BATCH)
            for group in range(j // 8, groups)
        }
        for group in range(groups):
            taken = (lanes >= first + start) & (lanes < first + start + BATCH)
            unit = jnp.where(lanes == index + (first + 8 * group), 1.0, 0.0)
            rows[group][0] = jnp.where(taken, unit, rows[group][0])
        for j in range(start, start + BATCH, 2):
            home, place = divmod(j, 8)
            a = down(columns[home, j], place)
            b = down(columns[home, j], place + 1)
            c = down(columns[home, j + 1], place + 1)
            minor = a * c - b * b
            over_a, over_minor = 1.0 / a, 1.0 / minor
            ratio = b * over_a
            pivots[home] = jnp.where(index == place, a, pivots[home])
            pivots[home] = jnp.where(index == place + 1, minor * over_a, pivots[home])
            first_factor, second_factor = {}, {}
            for group in range(home, groups):
                one = columns[group, j]
                two = columns[group, j + 1] * a - one * b
                if group == home:
                    one = jnp.where(index > place, one, 0.0)
                    two = jnp.where(index > place + 1, two, 0.0)
                first_factor[group] = one * over_a
                second_factor[group] = two * over_minor
            for m in range(j + 2, start + BATCH):
                value = down(columns[m // 8, j], m % 8)
                other = down(columns[m // 8, j + 1], m % 8) - ratio * value
                for group in range(m // 8, groups):
                    columns[group, m] = (
                        columns[group, m]
                        - first_factor[group] * value
                        - second_factor[group] * other
                    )
            for tile in range(len(rows[0])):
                value = down(rows[home][tile], place)
                other = down(rows[home][tile], place + 1) - ratio * value
                for group in first_factor:
                    rows[group][tile] = (
                        rows[group][tile]
                        - first_factor[group] * value
                        - second_factor[group] * other
                    )
    return pivots


def factor_inverse(gram_ref):
    size = gram_ref.shape[0]
    tiles = size // LANES
    groups = BLOCK // 8

    def tile_of(index):
        return slice(index * LANES, (index + 1) * LANES)

    for start in range(0, size, BLOCK):
        stop = start + BLOCK
        here = start // LANES
        order = [here] + [t for t in range(tiles) if t != here]
        rows = [
            [gram_ref[start + 8 * group : start + 8 * group + 8, tile_of(t)] for t in order]
            for group in range(groups)
        ]
        pivots = eliminate(rows, start % LANES)
        scaled = {t: [] for t in order}
        for group in range(groups):
            scale = lax.rsqrt(pivots[group])
            for t, value in zip(order, rows[group]):
                scaled[t].append(value * scale)
        stacked = [jnp.concatenate(scaled[t], axis=0) for t in range(tiles)]
        lanes = lax.broadcasted_iota(jnp.int32, (BLOCK, LANES), 1)
        done = jnp.where(lanes < stop - here * LANES, stacked[here], 0.0)
        for t in range(tiles):
            gram_ref[start:stop, tile_of(t)] = (
                stacked[t] if t < here else done if t == here else jnp.zeros_like(done)
            )
        if stop == size:
            break
        base = stop // LANES
        left = jnp.concatenate(stacked[base:], axis=1)
        product = dot(
            left_of(left, 0, 6), right_of(jnp.concatenate(stacked, axis=1), 6), ((0,), (0,))
        )[stop - base * LANES :]
        for t in range(tiles):
            before = gram_ref[stop:, tile_of(t)]
            if t == here:
                lanes = lax.broadcasted_iota(jnp.int32, before.shape, 1) + here * LANES
                before = jnp.where((lanes >= start) & (lanes < stop), 0.0, before)
            gram_ref[stop:, tile_of(t)] = before - product[:, tile_of(t)]


def factor_kernel(
    place_ref, own_ref, other_ref, rows_ref, left_ref, split_ref, unit_ref, root_ref,
    inverse_ref, packed_ref,
):
    core, chip, _ = place_of(place_ref)
    tall = LANES // SLOTS
    for side, ref in ((core, own_ref), (1 - core, other_ref)):
        for slot in range(SLOTS):
            chunk = jnp.bitwise_xor(chip, slot)
            row = pl.multiple_of(chunk * tall, 8)
            packed_ref[side, pl.ds(row, tall), :] = ref[slot, :tall, :]

            @pl.when(chunk == 0)
            def _(side=side, ref=ref, slot=slot):
                packed_ref[side, LANES:, :] = ref[slot, tall:, :]

    root = jnp.sqrt(unpack_gram(packed_ref, inverse_ref))
    root_ref[...] = jnp.broadcast_to(root, root_ref.shape)
    factor_inverse(inverse_ref)
    inverse = inverse_ref[...]
    left_ref[...] = left_of(inverse, 1)
    unit = dot(rows_ref[...], right_of(inverse, axis=1), ((1,), (1,)))
    split_ref[...] = left_of(unit, 1)
    unit_ref[...] = unit


def factor_of(place, own, other, panel_rows):
    rows = panel_rows.shape[0]
    width = panel_rows.shape[1] // 3
    return pl.pallas_call(
        factor_kernel,
        out_shape=(
            jax.ShapeDtypeStruct((width, 3 * width), BF16),
            jax.ShapeDtypeStruct((rows, 3 * width), BF16),
            struct(rows, width),
            struct(8, LANES),
        ),
        in_specs=[SMEM, VMEM, VMEM, VMEM],
        out_specs=(VMEM,) * 4,
        scratch_shapes=[
            pltpu.VMEM((width, width), F32),
            pltpu.VMEM((2, LANES + EXTRA, LANES), F32),
        ],
        cost_estimate=cost(6 * 10**9, 4 * rows * width),
        compiler_params=PARAMS,
        name="factor",
    )(place, own, other, panel_rows)


def rest_kernel(other, place_ref, live_ref, inverse_ref, split_ref, cross_ref, trail_ref, *refs):
    width = inverse_ref.shape[0]
    columns = trail_ref.shape[1]
    half = columns // 2
    core, chip, depth = place_of(place_ref)
    if other:
        *_, top_ref, rest_ref, top_scr, cross_scr, rest_scr, top_sem, rest_sem = refs
        side = 1 - core
    else:
        unit_ref, root_ref, *refs = refs
        top_ref, rest_ref, basis_ref, top_scr, cross_scr, rest_scr, top_sem, rest_sem, *refs = refs
        basis_scr, basis_sem = refs
        side = core
        basis_scr[...] = unit_ref[...] * root_ref[0:1, 0:1]
        copy_basis = pltpu.make_async_copy(basis_scr, basis_ref, basis_sem)
        copy_basis.start()
    start = pl.multiple_of(side * half, half)
    part = width // PARTS
    for slot in range(SLOTS):
        lane = pl.multiple_of(jnp.bitwise_xor(chip, slot) * LANES, LANES)
        for piece in range(PARTS):
            row = pl.multiple_of(jnp.bitwise_xor(depth, piece) * part, 8)
            cross_scr[pl.ds(row, part), pl.ds(lane, LANES)] = cross_ref[
                slot, piece * part : (piece + 1) * part, :
            ]
    top = dot(inverse_ref[...], right_of(cross_scr[...]))
    top_scr[...] = top
    wide = top_ref.shape[1]
    begin = place_ref[0] % (columns // wide) * wide
    mine = begin // half == side
    copy_top = pltpu.make_async_copy(
        top_scr.at[:, pl.ds(pl.multiple_of(begin % half, LANES), wide)], top_ref, top_sem
    )

    @pl.when(mine)
    def _():
        copy_top.start()

    rest_scr[...] = masked(trail_ref, live_ref, pl.ds(start, half)) - dot(
        split_ref[...], right_of(top)
    )
    copy_rest = pltpu.make_async_copy(rest_scr, rest_ref.at[:, pl.ds(start, half)], rest_sem)
    copy_rest.start()
    copy_rest.wait()

    @pl.when(mine)
    def _():
        copy_top.wait()

    if not other:
        copy_basis.wait()


def rest_of(other, place, live, inverse, split, cross, trail, wide, more):
    rows, columns = trail.shape
    width = inverse.shape[0]
    half = columns // 2
    basis = [] if other else [struct(rows, width)]
    return pl.pallas_call(
        functools.partial(rest_kernel, other),
        out_shape=[struct(width, wide), struct(rows, columns)] + basis,
        in_specs=[SMEM] * 2 + [VMEM] * 4 + [ANY if other else VMEM] * 2,
        out_specs=[ANY] * (2 + len(basis)),
        scratch_shapes=[
            pltpu.VMEM((width, half), F32),
            pltpu.VMEM((width, half), F32),
            pltpu.VMEM((rows, half), F32),
            pltpu.SemaphoreType.DMA,
            pltpu.SemaphoreType.DMA,
        ]
        + ([] if other else [pltpu.VMEM((rows, width), F32), pltpu.SemaphoreType.DMA]),
        input_output_aliases={6: 0, 7: 1} if other else {},
        cost_estimate=cost(6 * (rows + width) * width * half, 8 * rows * half),
        compiler_params=PARAMS,
        name="rest_other" if other else "rest_own",
    )(place, live, inverse, split, cross, trail, *more)


def swap(x):
    return lax.ppermute(x, "core", [(0, 1), (1, 0)])


def send(x, axes, size, shift):
    return lax.ppermute(x, axes, [(i, i ^ shift) for i in range(size)])


def tree(parts):
    return (parts[0] + parts[1]) + (parts[2] + parts[3])


def body(panel, trailing, live_rows):
    width, columns = panel.shape[1], trailing.shape[1]
    flat, deep = ("y", "x"), "z"
    wide = columns // (lax.axis_size("x") * 2)
    place = lax.axis_index(AXES)[None]
    tall, part = LANES // SLOTS + EXTRA, width // PARTS

    theirs, ours, panel_rows = products_of(place, live_rows, panel, trailing)
    order = [3, 1, 2, 0]
    arrived = {k: swap(theirs[k]) for k in order}
    pair = {k: ours[k] + arrived[k] for k in order}
    slots = [pair[0]] + [send(pair[k], flat, SLOTS, k) for k in range(1, SLOTS)]
    summed = tree(slots)
    gram = summed[:tall]
    pieces = [
        jnp.concatenate([gram, summed[tall + j * part : tall + (j + 1) * part]])
        for j in range(PARTS)
    ]
    pieces = [pieces[0]] + [send(pieces[j], deep, PARTS, j) for j in range(1, PARTS)]
    summed = tree(pieces)
    if lax.axis_size("far") > 1:
        summed = lax.psum(summed, "far")
    gram, cross = summed[:tall], summed[tall:]
    gram_own = jnp.stack([gram] + [send(gram, flat, SLOTS, k) for k in range(1, SLOTS)])
    cross = jnp.concatenate([cross, send(cross, deep, PARTS, 1)])
    cross = jnp.concatenate([cross, send(cross, deep, PARTS, 2)])
    cross_own = [cross] + [send(cross, flat, SLOTS, k) for k in range(1, SLOTS)]
    inverse, split, unit, root = factor_of(place, gram_own, swap(gram_own), panel_rows)
    *cross_own, inverse = lax.optimization_barrier((*cross_own, inverse))
    cross_own = jnp.stack(cross_own)
    cross_other = swap(cross_own)
    args = (place, live_rows, inverse, split)
    top, rest, basis = rest_of(False, *args, cross_own, trailing, wide, (unit, root))
    top, rest = rest_of(True, *args, cross_other, trailing, wide, (top, rest))
    return basis, top, rest


def solution(mesh):
    rows, subs = mesh.shape["rows"], mesh.shape["sub"]
    grid = Mesh(mesh.devices.reshape(rows // (2 * PARTS), PARTS, 2, subs // 2, 2), AXES)
    in_specs = (P(AXES, None), P(AXES, None), P(AXES))
    out_specs = (P(AXES, None), P(None, ("x", "core")), P(AXES, None))
    return jax.shard_map(
        body, mesh=grid, in_specs=in_specs, out_specs=out_specs, check_vma=False
    )
```

```python
import functools

import jax
import jax.numpy as jnp
from jax import lax
from jax.experimental import pallas as pl
from jax.experimental.pallas import tpu as pltpu
from jax.sharding import Mesh
from jax.sharding import PartitionSpec as P

AXES = ("far", "z", "y", "x", "core")
SLOTS = 4
PARTS = 4
F32 = jnp.float32
BF16 = jnp.bfloat16
LANES = 128
BLOCK = 32
BATCH = 16
STRIPS = 2
EXTRA = 8
SMEM = pl.BlockSpec(memory_space=pltpu.SMEM)
VMEM = pl.BlockSpec(memory_space=pltpu.VMEM)
ANY = pl.BlockSpec(memory_space=pl.ANY)
HBM = pl.BlockSpec(memory_space=pltpu.HBM)
PARAMS = pltpu.CompilerParams(vmem_limit_bytes=16 << 20)


def in_hbm(x):
    return pltpu.with_memory_space_constraint(x, pltpu.HBM)


def place_of(ref):
    number = ref[0]
    return number % 2, number // 2 % SLOTS, number // (2 * SLOTS) % PARTS


def parts_of(x):
    high = x.astype(BF16)
    rest = x - high.astype(F32)
    middle = rest.astype(BF16)
    return high, middle, (rest - middle.astype(F32)).astype(BF16)


def left_of(x, axis, count=3):
    a, b, c = parts_of(x)
    return jnp.concatenate([a, a, b, a, c, b][:count], axis=axis)


def right_of(x, count=3, axis=0):
    a, b, c = parts_of(x)
    return jnp.concatenate([a, b, a, c, a, b][:count], axis=axis)


def dot(left, right, contract=((1,), (0,))):
    return lax.dot_general(left, right, (contract, ((), ())), preferred_element_type=F32)


def masked(ref, live_ref, columns=slice(None)):
    rows = ref.shape[0]
    live = lax.broadcasted_iota(jnp.int32, (rows, 1), 0) < live_ref[0]
    return jnp.where(live, ref[:, columns], 0.0)


def struct(*shape):
    return jax.ShapeDtypeStruct(shape, F32)


def cost(flops, transferred):
    return pl.CostEstimate(flops=flops, bytes_accessed=transferred, transcendentals=0)


def place_products(place_ref, gram, cross, out_refs, cross_scr):
    width = cross.shape[0]
    _, chip, depth = place_of(place_ref)
    tall = LANES // SLOTS
    part = width // PARTS
    for tile in range(SLOTS):
        cross_scr[tile] = cross[:, tile * LANES : (tile + 1) * LANES]
    for slot in range(SLOTS):
        chunk = jnp.bitwise_xor(chip, slot)
        out_ref = out_refs[slot]
        out_ref[:tall, :] = gram[pl.ds(pl.multiple_of(chunk * tall, 8), tall), :]
        out_ref[tall : tall + EXTRA, :] = gram[LANES:, :]
        for piece in range(PARTS):
            at = pl.multiple_of(jnp.bitwise_xor(depth, piece) * part, 8)
            to = tall + EXTRA + piece * part
            out_ref[to : to + part, :] = cross_scr[chunk, pl.ds(at, part), :]


def triangle():
    shape = (LANES, LANES)
    row = lax.broadcasted_iota(jnp.int32, shape, 0)
    column = lax.broadcasted_iota(jnp.int32, shape, 1)
    return row, column


def pack_gram(gram, live, gram_ref):
    row, column = triangle()
    second = gram[LANES:, LANES:]
    gram_ref[0, :LANES, :] = gram[:LANES, LANES:]
    gram_ref[1, :LANES, :] = jnp.where(row <= column, gram[:LANES, :LANES], second)
    diagonal = jnp.sum(jnp.where(row == column, second, 0.0), axis=0, keepdims=True)
    count = jnp.full((EXTRA, LANES), live, jnp.int32).astype(F32)
    index = lax.broadcasted_iota(jnp.int32, (EXTRA, LANES), 0)
    for side in range(2):
        gram_ref[side, LANES:, :] = jnp.where(index == 0, diagonal, count)


def unpack_gram(packed_ref, gram_ref):
    row, column = triangle()
    packed = packed_ref[1, :LANES, :]
    turned = packed.T
    diagonal = packed_ref[1, LANES : LANES + 1, :]
    gram_ref[:LANES, :LANES] = jnp.where(row <= column, packed, turned)
    gram_ref[:LANES, LANES:] = packed_ref[0, :LANES, :]
    second = jnp.where(row > column, packed, turned)
    gram_ref[LANES:, LANES:] = jnp.where(row == column, diagonal, second)
    return packed_ref[1, LANES + 1 : LANES + 2, 0:1]


def other_kernel(
    place_ref, live_ref, panel_ref, trail_ref, *refs
):
    out_refs = refs[:SLOTS]
    left_ref, gram_ref, half_ref, panel_scr, cross_scr, trail_scr, *sems = refs[SLOTS:]
    panel_sem, trail_sem, half_sem = sems
    columns = trail_ref.shape[1]
    core = place_of(place_ref)[0]
    wide = columns // 2

    def columns_of(side):
        return trail_ref.at[:, pl.ds(pl.multiple_of(side * wide, LANES), wide)]

    copy_panel = pltpu.make_async_copy(panel_ref, panel_scr, panel_sem)
    copy_trail = pltpu.make_async_copy(columns_of(1 - core), trail_scr, trail_sem)
    copy_half = pltpu.make_async_copy(columns_of(core), half_ref, half_sem)
    copy_panel.start()
    copy_trail.start()
    copy_half.start()
    copy_panel.wait()
    rows = panel_scr.shape[0]
    panel = masked(panel_scr, live_ref)
    left = left_of(panel.T, 1)
    left_ref[...] = left
    high, middle, low = parts_of(panel)
    mixed = dot(left[:, : 2 * rows], jnp.concatenate([middle, low], axis=0))
    gram = dot(left[:, rows:], jnp.concatenate([high, middle], axis=0)) + (mixed + mixed.T)
    pack_gram(gram, live_ref[0], gram_ref)
    copy_trail.wait()
    cross = dot(left, right_of(masked(trail_scr, live_ref)))
    place_products(place_ref, gram_ref.at[1 - core], cross, out_refs, cross_scr)
    copy_half.wait()


def own_kernel(
    place_ref, live_ref, left_ref, gram_ref, half_ref, panel_ref, *refs
):
    *out_refs, rows_ref, cross_scr = refs
    cross = dot(left_ref[...], right_of(masked(half_ref, live_ref)))
    core = place_of(place_ref)[0]
    place_products(place_ref, gram_ref.at[core], cross, out_refs, cross_scr)
    rows_ref[...] = left_of(masked(panel_ref, live_ref), 1)


def products_of(place, live, panel, trail):
    rows, width = panel.shape
    columns = trail.shape[1]
    out = (struct(LANES // SLOTS + EXTRA + width, LANES),) * SLOTS
    work = cost(6 * rows * width * columns // 2, 2 * rows * columns)
    cross_scr = pltpu.VMEM((SLOTS, width, LANES), F32)
    outs = pl.pallas_call(
        other_kernel,
        out_shape=(
            *out,
            jax.ShapeDtypeStruct((width, 3 * rows), BF16),
            struct(2, LANES + EXTRA, LANES),
            struct(rows, columns // 2),
            struct(rows, width),
        ),
        in_specs=[SMEM, SMEM, HBM, HBM],
        out_specs=(VMEM,) * (SLOTS + 4),
        scratch_shapes=[cross_scr, pltpu.VMEM((rows, columns // 2), F32)]
        + [pltpu.SemaphoreType.DMA] * 3,
        cost_estimate=work,
        compiler_params=PARAMS,
        name="products_other",
    )(place, live, in_hbm(panel), in_hbm(trail))
    theirs, handed = outs[:SLOTS], outs[SLOTS:]
    *ours, panel_rows = pl.pallas_call(
        own_kernel,
        out_shape=(*out, jax.ShapeDtypeStruct((rows, 3 * width), BF16)),
        in_specs=[SMEM, SMEM] + [VMEM] * 4,
        out_specs=(VMEM,) * (SLOTS + 1),
        scratch_shapes=[cross_scr],
        cost_estimate=work,
        compiler_params=PARAMS,
        name="products_own",
    )(place, live, *handed)
    return theirs, ours, panel_rows


def across(x, lane):
    return jnp.broadcast_to(x[:, lane : lane + 1], (8, LANES))


def down(x, row):
    return jnp.broadcast_to(x[row : row + 1, :], (8, LANES))


def eliminate(rows, first):
    groups = len(rows)
    index = lax.broadcasted_iota(jnp.int32, (8, LANES), 0)
    lanes = lax.broadcasted_iota(jnp.int32, (8, LANES), 1)
    pivots = [jnp.ones((8, LANES), F32) for _ in range(groups)]
    for start in range(0, BLOCK, BATCH):
        columns = {
            (group, j): across(rows[group][0], first + j)
            for j in range(start, start + BATCH)
            for group in range(j // 8, groups)
        }
        for group in range(groups):
            taken = (lanes >= first + start) & (lanes < first + start + BATCH)
            unit = jnp.where(lanes == index + (first + 8 * group), 1.0, 0.0)
            rows[group][0] = jnp.where(taken, unit, rows[group][0])
        for j in range(start, start + BATCH, 2):
            home, place = divmod(j, 8)
            a = down(columns[home, j], place)
            b = down(columns[home, j], place + 1)
            c = down(columns[home, j + 1], place + 1)
            minor = a * c - b * b
            over_a, over_minor = 1.0 / a, 1.0 / minor
            ratio = b * over_a
            pivots[home] = jnp.where(index == place, a, pivots[home])
            pivots[home] = jnp.where(index == place + 1, minor * over_a, pivots[home])
            first_factor, second_factor = {}, {}
            for group in range(home, groups):
                one = columns[group, j]
                two = columns[group, j + 1] * a - one * b
                if group == home:
                    one = jnp.where(index > place, one, 0.0)
                    two = jnp.where(index > place + 1, two, 0.0)
                first_factor[group] = one * over_a
                second_factor[group] = two * over_minor
            for m in range(j + 2, start + BATCH):
                value = down(columns[m // 8, j], m % 8)
                other = down(columns[m // 8, j + 1], m % 8) - ratio * value
                for group in range(m // 8, groups):
                    columns[group, m] = (
                        columns[group, m]
                        - first_factor[group] * value
                        - second_factor[group] * other
                    )
            for tile in range(len(rows[0])):
                value = down(rows[home][tile], place)
                other = down(rows[home][tile], place + 1) - ratio * value
                for group in first_factor:
                    rows[group][tile] = (
                        rows[group][tile]
                        - first_factor[group] * value
                        - second_factor[group] * other
                    )
    return pivots


def factor_inverse(gram_ref):
    size = gram_ref.shape[0]
    tiles = size // LANES
    groups = BLOCK // 8

    def tile_of(index):
        return slice(index * LANES, (index + 1) * LANES)

    for start in range(0, size, BLOCK):
        stop = start + BLOCK
        here = start // LANES
        order = [here] + [t for t in range(tiles) if t != here]
        rows = [
            [gram_ref[start + 8 * group : start + 8 * group + 8, tile_of(t)] for t in order]
            for group in range(groups)
        ]
        pivots = eliminate(rows, start % LANES)
        scaled = {t: [] for t in order}
        for group in range(groups):
            scale = lax.rsqrt(pivots[group])
            for t, value in zip(order, rows[group]):
                scaled[t].append(value * scale)
        stacked = [jnp.concatenate(scaled[t], axis=0) for t in range(tiles)]
        lanes = lax.broadcasted_iota(jnp.int32, (BLOCK, LANES), 1)
        done = jnp.where(lanes < stop - here * LANES, stacked[here], 0.0)
        for t in range(tiles):
            gram_ref[start:stop, tile_of(t)] = (
                stacked[t] if t < here else done if t == here else jnp.zeros_like(done)
            )
        if stop == size:
            break
        base = stop // LANES
        left = jnp.concatenate(stacked[base:], axis=1)
        product = dot(
            left_of(left, 0, 6), right_of(jnp.concatenate(stacked, axis=1), 6), ((0,), (0,))
        )[stop - base * LANES :]
        for t in range(tiles):
            before = gram_ref[stop:, tile_of(t)]
            if t == here:
                lanes = lax.broadcasted_iota(jnp.int32, before.shape, 1) + here * LANES
                before = jnp.where((lanes >= start) & (lanes < stop), 0.0, before)
            gram_ref[stop:, tile_of(t)] = before - product[:, tile_of(t)]


def factor_kernel(
    place_ref, own_ref, other_ref, rows_ref, left_ref, split_ref, unit_ref, root_ref,
    inverse_ref, packed_ref,
):
    core, chip, _ = place_of(place_ref)
    tall = LANES // SLOTS
    for side, ref in ((core, own_ref), (1 - core, other_ref)):
        for slot in range(SLOTS):
            chunk = jnp.bitwise_xor(chip, slot)
            row = pl.multiple_of(chunk * tall, 8)
            packed_ref[side, pl.ds(row, tall), :] = ref[slot, :tall, :]

            @pl.when(chunk == 0)
            def _(side=side, ref=ref, slot=slot):
                packed_ref[side, LANES:, :] = ref[slot, tall:, :]

    root = jnp.sqrt(unpack_gram(packed_ref, inverse_ref))
    root_ref[...] = jnp.broadcast_to(root, root_ref.shape)
    factor_inverse(inverse_ref)
    inverse = inverse_ref[...]
    left_ref[...] = left_of(inverse, 1)
    unit = dot(rows_ref[...], right_of(inverse, axis=1), ((1,), (1,)))
    split_ref[...] = left_of(unit, 1)
    unit_ref[...] = unit


def factor_of(place, own, other, panel_rows):
    rows = panel_rows.shape[0]
    width = panel_rows.shape[1] // 3
    return pl.pallas_call(
        factor_kernel,
        out_shape=(
            jax.ShapeDtypeStruct((width, 3 * width), BF16),
            jax.ShapeDtypeStruct((rows, 3 * width), BF16),
            struct(rows, width),
            struct(8, LANES),
        ),
        in_specs=[SMEM, VMEM, VMEM, VMEM],
        out_specs=(VMEM,) * 4,
        scratch_shapes=[
            pltpu.VMEM((width, width), F32),
            pltpu.VMEM((2, LANES + EXTRA, LANES), F32),
        ],
        cost_estimate=cost(6 * 10**9, 4 * rows * width),
        compiler_params=PARAMS,
        name="factor",
    )(place, own, other, panel_rows)


def rest_kernel(other, place_ref, live_ref, inverse_ref, split_ref, cross_ref, trail_ref, *refs):
    width = inverse_ref.shape[0]
    columns = trail_ref.shape[1]
    half = columns // 2
    core, chip, depth = place_of(place_ref)
    if other:
        *_, top_ref, rest_ref, top_scr, cross_scr, rest_scr, top_sem, rest_sem = refs
        side = 1 - core
    else:
        unit_ref, root_ref, *refs = refs
        top_ref, rest_ref, basis_ref, top_scr, cross_scr, rest_scr, top_sem, rest_sem, *refs = refs
        basis_scr, basis_sem = refs
        side = core
        basis_scr[...] = unit_ref[...] * root_ref[0:1, 0:1]
        copy_basis = pltpu.make_async_copy(basis_scr, basis_ref, basis_sem)
        copy_basis.start()
    start = pl.multiple_of(side * half, half)
    part = width // PARTS
    for slot in range(SLOTS):
        lane = pl.multiple_of(jnp.bitwise_xor(chip, slot) * LANES, LANES)
        for piece in range(PARTS):
            row = pl.multiple_of(jnp.bitwise_xor(depth, piece) * part, 8)
            cross_scr[pl.ds(row, part), pl.ds(lane, LANES)] = cross_ref[
                slot, piece * part : (piece + 1) * part, :
            ]
    top = dot(inverse_ref[...], right_of(cross_scr[...]))
    top_scr[...] = top
    wide = top_ref.shape[1]
    begin = place_ref[0] % (columns // wide) * wide
    mine = begin // half == side
    copy_top = pltpu.make_async_copy(
        top_scr.at[:, pl.ds(pl.multiple_of(begin % half, LANES), wide)], top_ref, top_sem
    )

    @pl.when(mine)
    def _():
        copy_top.start()

    right = right_of(top)
    trail = masked(trail_ref, live_ref, pl.ds(start, half))
    height = rest_scr.shape[0] // STRIPS
    copies = []
    for k in range(STRIPS):
        at = slice(k * height, (k + 1) * height)
        rest_scr[at, :] = trail[at] - dot(split_ref[at, :], right)
        copies.append(
            pltpu.make_async_copy(
                rest_scr.at[at, :], rest_ref.at[at, pl.ds(start, half)], rest_sem.at[k]
            )
        )
        copies[k].start()
    for copy in copies:
        copy.wait()

    @pl.when(mine)
    def _():
        copy_top.wait()

    if not other:
        copy_basis.wait()


def rest_of(other, place, live, inverse, split, cross, trail, wide, more):
    rows, columns = trail.shape
    width = inverse.shape[0]
    half = columns // 2
    basis = [] if other else [struct(rows, width)]
    return pl.pallas_call(
        functools.partial(rest_kernel, other),
        out_shape=[struct(width, wide), struct(rows, columns)] + basis,
        in_specs=[SMEM] * 2 + [VMEM] * 4 + [ANY if other else VMEM] * 2,
        out_specs=[ANY] * (2 + len(basis)),
        scratch_shapes=[
            pltpu.VMEM((width, half), F32),
            pltpu.VMEM((width, half), F32),
            pltpu.VMEM((rows, half), F32),
            pltpu.SemaphoreType.DMA,
            pltpu.SemaphoreType.DMA((STRIPS,)),
        ]
        + ([] if other else [pltpu.VMEM((rows, width), F32), pltpu.SemaphoreType.DMA]),
        input_output_aliases={6: 0, 7: 1} if other else {},
        cost_estimate=cost(6 * (rows + width) * width * half, 8 * rows * half),
        compiler_params=PARAMS,
        name="rest_other" if other else "rest_own",
    )(place, live, inverse, split, cross, trail, *more)


def swap(x):
    return lax.ppermute(x, "core", [(0, 1), (1, 0)])


def send(x, axes, size, shift):
    return lax.ppermute(x, axes, [(i, i ^ shift) for i in range(size)])


def tree(parts):
    return (parts[0] + parts[1]) + (parts[2] + parts[3])


def body(panel, trailing, live_rows):
    width, columns = panel.shape[1], trailing.shape[1]
    flat, deep = ("y", "x"), "z"
    wide = columns // (lax.axis_size("x") * 2)
    place = lax.axis_index(AXES)[None]
    tall, part = LANES // SLOTS + EXTRA, width // PARTS

    theirs, ours, panel_rows = products_of(place, live_rows, panel, trailing)
    order = [3, 1, 2, 0]
    arrived = {k: swap(theirs[k]) for k in order}
    pair = {k: ours[k] + arrived[k] for k in order}
    slots = [pair[0]] + [send(pair[k], flat, SLOTS, k) for k in range(1, SLOTS)]
    summed = tree(slots)
    gram = summed[:tall]
    pieces = [
        jnp.concatenate([gram, summed[tall + j * part : tall + (j + 1) * part]])
        for j in range(PARTS)
    ]
    pieces = [pieces[0]] + [send(pieces[j], deep, PARTS, j) for j in range(1, PARTS)]
    summed = tree(pieces)
    if lax.axis_size("far") > 1:
        summed = lax.psum(summed, "far")
    gram, cross = summed[:tall], summed[tall:]
    gram_own = jnp.stack([gram] + [send(gram, flat, SLOTS, k) for k in range(1, SLOTS)])
    cross = jnp.concatenate([cross, send(cross, deep, PARTS, 1)])
    cross = jnp.concatenate([cross, send(cross, deep, PARTS, 2)])
    cross_own = [cross] + [send(cross, flat, SLOTS, k) for k in range(1, SLOTS)]
    inverse, split, unit, root = factor_of(place, gram_own, swap(gram_own), panel_rows)
    *cross_own, inverse = lax.optimization_barrier((*cross_own, inverse))
    cross_own = jnp.stack(cross_own)
    cross_other = swap(cross_own)
    args = (place, live_rows, inverse, split)
    top, rest, basis = rest_of(False, *args, cross_own, trailing, wide, (unit, root))
    top, rest = rest_of(True, *args, cross_other, trailing, wide, (top, rest))
    return basis, top, rest


def solution(mesh):
    rows, subs = mesh.shape["rows"], mesh.shape["sub"]
    grid = Mesh(mesh.devices.reshape(rows // (2 * PARTS), PARTS, 2, subs // 2, 2), AXES)
    in_specs = (P(AXES, None), P(AXES, None), P(AXES))
    out_specs = (P(AXES, None), P(None, ("x", "core")), P(AXES, None))
    return jax.shard_map(
        body, mesh=grid, in_specs=in_specs, out_specs=out_specs, check_vma=False
    )
```
